32 devices in a mesh: stream: 8 (over z, y), span: 4 (over x, core).
Axes of the slice: x: 2, y: 2, z: 4, core: 2. Of those that a mesh axis runs over, the one named last changes fastest.
Arguments:
- records: bfloat16 [32, 9, 4, 512], P(('stream', 'span')), may hold values from -6 to 6
- cells: int32 [32, 9, 512], P(('stream', 'span')), may hold values from 0 to 524287
- counts: int32 [32, 9], P(('stream', 'span')), may hold values from 0 to 512, as said below
- background: float32 [3, 512], replicated, may hold values from -6 to 6
- field: float32 [3, 512], replicated, may hold values from -6 to 6
Outputs:
- density: float32 [4, 512, 64, 512], P(None, 'stream', 'span')
- velocity: float32 [32, 9, 3, 512], P(('stream', 'span'))
The draws below stay inside these ranges and needn't reach their ends.
Inputs may be any that keep to these rules, and one draw needn't show every extreme that they name: counts[o, d] live records of device o go in direction d: slots j < counts[o, d] are live, the others unused; counts is 0 where the destination span index lies beyond a wall. In every draw some device receives 512 live records from every device that sends to it.
All inputs are finite; a program needn't handle non-finite values.
Results may differ from the reference program's by a relative error of at most 0.00105.
Values may be sent and summed in bfloat16 or wider, within the bound.
No kernel may reach another device: no remote copies, remote signals or barrier semaphores. Data moves between devices by JAX's collectives and lax.ppermute only.
A program may use at most 192 MiB of HBM per device.

```python
import jax
import jax.numpy as jnp
from jax import lax

CX = 64
CY = 16
NZ = 512
CAP = 512
NX = 512
NY = 64
N_STREAM = 8
N_SPAN = 4
DEVICES = 32


def draw_counts(key, part):
    devices = N_STREAM * N_SPAN
    first, second, third = jax.random.split(key, 3)
    left = jax.random.randint(first, (devices, 9), CAP // 2, CAP + 1)
    right = jax.random.randint(second, (devices, 9), CAP // 2, CAP + 1)
    load = left * right // CAP
    ranks = jnp.arange(devices, dtype=jnp.int32)
    stream_of = ranks // N_SPAN
    span_of = ranks % N_SPAN
    direction_ids = jnp.arange(9, dtype=jnp.int32)
    step_stream = direction_ids // 3 - 1
    step_span = direction_ids % 3 - 1
    dest_span = span_of[:, None] + step_span[None, :]
    dest_stream = (stream_of[:, None] + step_stream[None, :]) % N_STREAM
    inside = (dest_span >= 0) & (dest_span < N_SPAN)
    target = jax.random.randint(third, (), 0, devices)
    load = jnp.where(dest_stream * N_SPAN + dest_span == target, CAP, load)
    return jnp.where(inside, load, 0).astype(jnp.int32)


def plant(drawn, rng, least, largest):
    extent = drawn.shape
    index_at = [jax.random.randint(jax.random.fold_in(rng, axis), (), 0, extent[axis]) for axis in range(len(extent))]
    drawn = drawn.at[tuple(index_at)].set(least)
    longest = extent.index(max(extent))
    index_at[longest] = (index_at[longest] + 1) % extent[longest]
    return drawn.at[tuple(index_at)].set(largest)


def block_levels(stream_key, shape, cuts, low, top_value):
    gain, own = 1.0, jax.random.fold_in(stream_key, 6)
    for dim, parts in cuts:
        steps = jnp.exp(jax.random.uniform(jax.random.fold_in(own, dim), (parts,), jnp.float32, low / len(cuts), top_value / len(cuts)))
        gain = gain * jnp.repeat(steps, shape[dim] // parts).reshape([-1 if axis == dim else 1 for axis in range(len(shape))])
    return gain


def noise(stream_key, dims, width, reach, cuts=(), kind=jnp.bfloat16):
    result = jax.random.normal(stream_key, dims, jnp.float32) * width
    if len(cuts) > 0:
        result = block_levels(stream_key, dims, cuts, -0.22, 0.18) * result
    return jnp.clip(result, min=-reach, max=reach).astype(kind)


def setup_inputs(seed: int = 0) -> dict:
    arg_keys = jax.random.split(jax.random.key(seed), 6)
    records = noise(arg_keys[0], (DEVICES, 9, 4, CAP), 1.0, 6.0, ((0, 32),))
    cells = plant(jax.random.randint(arg_keys[1], (DEVICES, 9, CAP), 0, CX * CY * NZ), jax.random.fold_in(arg_keys[1], 1), 0, (CX * CY * NZ) - 1).astype(jnp.int32)
    counts = draw_counts(jax.random.fold_in(arg_keys[5], 71), 0)
    background = noise(arg_keys[3], (3, NZ), 1.0, 6.0, (), jnp.float32)
    field = noise(arg_keys[4], (3, NZ), 1.0, 6.0, (), jnp.float32)
    return {"records": records, "cells": cells, "counts": counts, "background": background, "field": field}


spread_width = 12.5


def kernel_taps():
    offsets = jnp.arange(-6, 7).astype(jnp.float32)
    return jnp.exp(-offsets * offsets / spread_width)


def filter_valid(values, taps, axis):
    length = values.shape[axis] - 12
    total = taps[0] * lax.slice_in_dim(values, 0, length, axis=axis)
    for offset in range(1, 13):
        total = total + taps[offset] * lax.slice_in_dim(values, offset, offset + length, axis=axis)
    return total


def smooth_grid(values, taps):
    padded = jnp.pad(values, ((0, 0), (0, 0), (0, 0), (6, 6)))
    values = filter_valid(padded, taps, 3)
    padded = jnp.pad(values, ((0, 0), (6, 6), (0, 0), (0, 0)), mode="wrap")
    values = filter_valid(padded, taps, 1)
    padded = jnp.pad(values, ((0, 0), (0, 0), (6, 6), (0, 0)))
    return filter_valid(padded, taps, 2)


def reference(records, cells, counts, background, field):
    devices = N_STREAM * N_SPAN
    cap = records.shape[3]
    ranks = jnp.arange(devices, dtype=jnp.int32)
    stream_of = ranks // N_SPAN
    span_of = ranks % N_SPAN
    direction_ids = jnp.arange(9, dtype=jnp.int32)
    step_stream = direction_ids // 3 - 1
    step_span = direction_ids % 3 - 1
    source_stream = (stream_of[:, None] - step_stream[None, :]) % N_STREAM
    source_span = span_of[:, None] - step_span[None, :]
    inside = (source_span >= 0) & (source_span < N_SPAN)
    source = source_stream * N_SPAN + jnp.clip(source_span, 0, N_SPAN - 1)
    got_count = jnp.where(inside, counts[source, direction_ids[None, :]], 0)
    slots = jnp.arange(cap, dtype=jnp.int32)
    live = slots[None, None, :] < got_count[:, :, None]
    got_records = records[source, direction_ids[None, :]].astype(jnp.float32)
    got_cells = cells[source, direction_ids[None, :]]
    local_x = got_cells // (CY * NZ)
    local_y = (got_cells // NZ) % CY
    local_z = got_cells % NZ
    global_x = stream_of[:, None, None] * CX + local_x
    global_y = span_of[:, None, None] * CY + local_y
    flat = ((global_x * NY + global_y) * NZ + local_z).astype(jnp.int32)
    values = jnp.where(live[:, :, None, :], got_records, jnp.float32(0.0))
    values = jnp.transpose(values, (2, 0, 1, 3)).reshape(4, -1)
    binned = jnp.zeros((4, NX * NY * NZ), jnp.float32).at[:, flat.reshape(-1)].add(values)
    binned = binned.reshape(4, NX, NY, NZ)
    raw_taps = kernel_taps()
    unit_taps = raw_taps / jnp.sum(raw_taps)
    spread = smooth_grid(binned, raw_taps)
    charge = spread[3]
    forces = spread[:3] + charge[None] * field[:, None, None, :]
    density = jnp.concatenate([forces, charge[None]], axis=0)
    flow = background[:, None, None, :] + forces
    smooth = smooth_grid(flow, unit_taps).reshape(3, -1)
    sampled = jnp.take(smooth, flat.reshape(-1), axis=1).reshape(3, devices, 9, cap)
    sampled = jnp.where(live[None], sampled, jnp.float32(0.0))
    velocity = jnp.transpose(sampled, (1, 2, 0, 3))
    return density, velocity
```

```python
import functools

import jax
import jax.numpy as jnp
from jax import lax
from jax.experimental import pallas as pl
from jax.experimental.pallas import tpu as pltpu
from jax.sharding import PartitionSpec as P

CX = 64
CY = 16
NZ = 512
REACH = 6
TILE = 256
BX = 8
NB = 10
BP = BX * CY
FAR = 255.0
ROWS = 16

spread_width = 12.5


def kernel_taps():
    offsets = jnp.arange(-6, 7).astype(jnp.float32)
    return jnp.exp(-offsets * offsets / spread_width)


def gauss(d):
    return jnp.where(jnp.abs(d) < REACH + 0.5, jnp.exp(d * d * (-1.0 / spread_width)), 0.0)


def hi_lo(v):
    hi = v.astype(jnp.bfloat16)
    lo = (v - hi.astype(jnp.float32)).astype(jnp.bfloat16)
    return hi, lo


def columns(xt, pick):
    return lax.dot_general(
        xt.astype(jnp.bfloat16), pick, (((0,), (0,)), ((), ())), preferred_element_type=jnp.float32
    )


def x_filtered(load, taps, count):
    outs = []
    ins = [load(i) for i in range(count + 12)]
    for o in range(count):
        total = taps[6] * ins[o + 6]
        for k in range(1, 7):
            total = total + taps[6 + k] * (ins[o + 6 - k] + ins[o + 6 + k])
        outs.append(total)
    return outs


def spread_kernel(lo_ref, hi_ref, taps_ref, tab_ref, pick_ref, field_ref, out_ref, acc, amat, zmat):
    step = pl.program_id(0)

    @pl.when(step == 0)
    def _():
        def clear(i, _):
            acc[i] = jnp.zeros(acc.shape[1:], jnp.float32)
            return 0

        lax.fori_loop(0, NB, clear, 0)

        def tile(i, _):
            first, last = lo_ref[i], hi_ref[i]

            @pl.when(first <= last)
            def _():
                xt = tab_ref[i]
                zrep = columns(xt, pick_ref[...])
                lane = lax.broadcasted_iota(jnp.int32, (TILE, 128), 1).astype(jnp.float32)
                for q in range(NZ // 128):
                    g = gauss(lane + (128.0 * q) - zrep)
                    hi, lo = hi_lo(g)
                    cols = slice(128 * q, 128 * (q + 1))
                    zmat[0:TILE, cols] = hi
                    zmat[TILE : 2 * TILE, cols] = hi
                    zmat[2 * TILE : 3 * TILE, cols] = lo
                ypl = lax.broadcasted_iota(jnp.int32, (CY, TILE), 0).astype(jnp.float32)
                gy = gauss(ypl - xt[5:6, :])
                parts = [hi_lo(gy * xt[c : c + 1, :]) for c in range(4)]

                def bucket(b, _):
                    for xx in range(BX):
                        at = (b * BX + xx).astype(jnp.float32)
                        m = jnp.where(xt[4:5, :] == at, 1.0, 0.0)
                        m = jnp.broadcast_to(m, (CY, TILE)).astype(jnp.bfloat16)
                        for c in range(4):
                            rows = slice(c * BP + xx * CY, c * BP + (xx + 1) * CY)
                            hi = parts[c][0] * m
                            amat[rows, 0:TILE] = hi
                            amat[rows, TILE : 2 * TILE] = parts[c][1] * m
                            amat[rows, 2 * TILE : 3 * TILE] = hi
                    acc[b] += jnp.dot(amat[...], zmat[...], preferred_element_type=jnp.float32)
                    return 0

                lax.fori_loop(first, last + 1, bucket, 0)

            return 0

        lax.fori_loop(0, tab_ref.shape[0], tile, 0)

    @pl.when(step > 0)
    def _():
        b = step - 1
        taps = [taps_ref[k] for k in range(13)]

        def chunk(j, _):
            cols = pl.ds(pl.multiple_of(j * 128, 128), 128)
            charge = None
            for c in (3, 0, 1, 2):

                def load(i, c=c):
                    start = c * BP + (i % BX) * CY
                    return acc[b + i // BX, start : start + CY, cols]

                outs = x_filtered(load, taps, BX)
                if c == 3:
                    charge = outs
                else:
                    f = field_ref[c : c + 1, cols]
                    outs = [v + q * f for v, q in zip(outs, charge)]
                for o in range(BX):
                    out_ref[c, o, :, cols] = outs[o]
            return 0

        lax.fori_loop(0, NZ // 128, chunk, 0)


def sample_kernel(
    lo_ref, hi_ref, taps_ref, tab_ref, pick_ref, ground_ref, dens_ref, out_ref, flow, fmat, gathered, scale_ref
):
    step = pl.program_id(0)
    last_step = pl.num_programs(0) - 1

    @pl.when(step == 0)
    def _():
        def clear(i, _):
            flow[:, i] = jnp.zeros((3, CY, NZ), jnp.float32)
            flow[:, 12 + CX + i] = jnp.zeros((3, CY, NZ), jnp.float32)
            return 0

        lax.fori_loop(0, 12, clear, 0)
        for i in range(12 + CX + 12, flow.shape[1]):
            flow[:, i] = jnp.zeros((3, CY, NZ), jnp.float32)

    @pl.when(step < last_step)
    def _():
        for c in range(3):
            g = ground_ref[c : c + 1, :]
            for i in range(BX):
                flow[c, 12 + step * BX + i] = dens_ref[c, i] + g

    @pl.when(step == last_step)
    def _():
        taps = [taps_ref[k] for k in range(13)]

        def block(b, _):
            for c in range(3):

                def chunk(j, _, c=c):
                    cols = pl.ds(pl.multiple_of(j * 128, 128), 128)
                    dest = pl.ds(pl.multiple_of(c * NZ + j * 128, 128), 128)
                    outs = x_filtered(lambda i: flow[c, b * BX + i, :, cols], taps, BX)
                    for o in range(BX):
                        hi, lo = hi_lo(outs[o])
                        fmat[b, o * CY : (o + 1) * CY, dest] = hi
                        fmat[b, BP + o * CY : BP + (o + 1) * CY, dest] = lo
                        fmat[b, 2 * BP + o * CY : 2 * BP + (o + 1) * CY, dest] = hi
                    return 0

                lax.fori_loop(0, NZ // 128, chunk, 0)
            return 0

        lax.fori_loop(0, NB, block, 0)
        scale = scale_ref[0]

        def tile(i, _):
            first, last = lo_ref[i], hi_ref[i]

            @pl.when(first > last)
            def _():
                out_ref[i] = jnp.zeros((8, TILE), jnp.float32)

            @pl.when(first <= last)
            def _():
                xt = tab_ref[i]
                cols = columns(xt, pick_ref[...])
                xrep, yrep, zrep = (cols[:, 128 * k : 128 * (k + 1)] for k in (2, 1, 0))
                lane_i = lax.broadcasted_iota(jnp.int32, (TILE, 128), 1)
                lane = lane_i.astype(jnp.float32)
                xpl = (lane_i // CY).astype(jnp.float32)
                ypl = (lane_i % CY).astype(jnp.float32)
                wy = gauss(ypl - yrep) * scale
                gathered[...] = jnp.zeros(gathered.shape, jnp.float32)

                def bucket(b, _):
                    a = jnp.where(xrep == xpl + (b * BX).astype(jnp.float32), wy, 0.0)
                    hi, lo = hi_lo(a)
                    full = jnp.concatenate([hi, hi, lo], axis=1)
                    gathered[...] += jnp.dot(full, fmat[b], preferred_element_type=jnp.float32)
                    return 0

                lax.fori_loop(first, last + 1, bucket, 0)
                sums = [None] * 3
                for q in range(NZ // 128):
                    wz = gauss(lane + (128.0 * q) - zrep) * scale
                    for c in range(3):
                        t = gathered[:, c * NZ + 128 * q : c * NZ + 128 * (q + 1)] * wz
                        sums[c] = t if sums[c] is None else sums[c] + t
                ones = jnp.ones((8, 256), jnp.bfloat16)
                for c in range(3):
                    hi, lo = hi_lo(sums[c])
                    both = jnp.concatenate([hi, lo], axis=1)
                    row = lax.dot_general(
                        ones, both, (((1,), (1,)), ((), ())), preferred_element_type=jnp.float32
                    )
                    out_ref[i, c : c + 1, :] = row[0:1, :]

            return 0

        lax.fori_loop(0, tab_ref.shape[0], tile, 0)


def smem():
    return pl.BlockSpec(memory_space=pltpu.SMEM)


def whole(shape):
    return pl.BlockSpec(shape, lambda i: (0,) * len(shape))


def spread_call(lo, hi, taps, table, pick, field):
    n = table.shape[0]
    steps = CX // BX
    return pl.pallas_call(
        spread_kernel,
        grid=(steps + 1,),
        in_specs=[smem(), smem(), smem(), whole(table.shape), whole(pick.shape), whole(field.shape)],
        out_specs=pl.BlockSpec((4, BX, CY, NZ), lambda i: (0, jnp.maximum(i - 1, 0), 0, 0)),
        out_shape=jax.ShapeDtypeStruct((4, CX, CY, NZ), jnp.float32),
        scratch_shapes=[
            pltpu.VMEM((NB, 4 * BP, NZ), jnp.float32),
            pltpu.VMEM((4 * BP, 3 * TILE), jnp.bfloat16),
            pltpu.VMEM((3 * TILE, NZ), jnp.bfloat16),
        ],
        compiler_params=pltpu.CompilerParams(vmem_limit_bytes=56 << 20),
        name="spread",
    )(lo, hi, taps, table, pick, field)


def sample_call(lo, hi, taps, table, pick, ground, density, scale):
    n = table.shape[0]
    steps = CX // BX
    return pl.pallas_call(
        sample_wrapped,
        grid=(steps + 1,),
        in_specs=[
            smem(),
            smem(),
            smem(),
            whole(table.shape),
            whole(pick.shape),
            whole(ground.shape),
            pl.BlockSpec((3, BX, CY, NZ), lambda i: (0, jnp.minimum(i, steps - 1), 0, 0)),
            smem(),
        ],
        out_specs=whole((n, 8, TILE)),
        out_shape=jax.ShapeDtypeStruct((n, 8, TILE), jnp.float32),
        scratch_shapes=[
            pltpu.VMEM((3, NB * BX + 12, CY, NZ), jnp.float32),
            pltpu.VMEM((NB, 3 * BP, 3 * NZ), jnp.bfloat16),
            pltpu.VMEM((TILE, 3 * NZ), jnp.float32),
        ],
        compiler_params=pltpu.CompilerParams(vmem_limit_bytes=56 << 20),
        name="sample",
    )(lo, hi, taps, table, pick, ground, density, scale)


def sample_wrapped(*refs):
    ins = refs[:8]
    sample_kernel(*ins[:7], *refs[8:], ins[7])


def ring(value, steps):
    count = lax.axis_size("stream")
    return lax.ppermute(value, "stream", [(i, (i + steps) % count) for i in range(count)])


def line(value, steps):
    count = lax.axis_size("span")
    first, last = max(0, -steps), min(count, count - steps)
    return lax.ppermute(value, "span", [(i, i + steps) for i in range(first, last)])


def on_device(records, cells, counts, background, field):
    cap = records.shape[3]
    total = 9 * cap
    tiles = total // TILE
    bf16, f32 = jnp.bfloat16, jnp.float32
    slots = jnp.arange(cap, dtype=jnp.int32)
    live = slots[None, :] < counts[0][:, None]
    cell = cells[0]
    z = cell % NZ
    x = jnp.where(live, cell // (CY * NZ), 255)
    y = (cell // NZ) % CY
    places = jnp.stack([x, y, z // 16, z % 16], axis=1).astype(bf16)
    outgoing = jnp.concatenate([records[0], places], axis=1).reshape(3, 3, 8, cap)
    dead = jnp.zeros((8,), bf16).at[4].set(255)[:, None]
    outgoing = jnp.stack([ring(outgoing[0], -1), outgoing[1], ring(outgoing[2], 1)])
    me = lax.axis_index("span")
    spans = lax.axis_size("span")
    has_low, has_high = me > 0, me < spans - 1
    from_high = jnp.where(has_high, line(outgoing[:, 0], -1), dead)
    from_low = jnp.where(has_low, line(outgoing[:, 2], 1), dead)
    inbound = jnp.stack([from_high, outgoing[:, 1], from_low], axis=1)
    inbound = inbound.transpose(2, 0, 1, 3).reshape(8, total)

    gi = inbound[4:].astype(jnp.int32)
    gx, gy, gz = gi[0], gi[1], gi[2] * 16 + gi[3]
    klass = (gy >= REACH).astype(jnp.int32) + (gy >= CY - REACH)
    klass = jnp.where(gx > 200, 3, klass)
    key = ((klass * 256 + gx) * CY + gy) * NZ + gz
    order = jnp.arange(total, dtype=jnp.int32)
    key, order, *vals = lax.sort((key, order) + tuple(inbound[c].astype(f32) for c in range(4)), num_keys=1)
    sz = key % NZ
    packed = jnp.stack(
        vals
        + [
            v.astype(f32)
            for v in (key // (CY * NZ) % 256, key // NZ % CY, sz // 16, sz % 16)
        ]
    ).astype(bf16)

    low = jnp.where(has_low, line(packed, 1), dead)
    high = jnp.where(has_high, line(packed, -1), dead)
    three = jnp.stack([low, packed, high])
    arrays = jnp.stack([ring(three, 1), three, ring(three, -1)]).astype(f32)
    shift = jnp.arange(-1, 2, dtype=f32)
    ax = arrays[:, :, 4]
    ax = jnp.where(ax > 200, FAR, ax + (CX * shift[:, None, None] + REACH))
    ay = arrays[:, :, 5] + CY * shift[None, :, None]
    table = jnp.concatenate(
        [arrays[:, :, :4], ax[:, :, None], ay[:, :, None], arrays[:, :, 6:], jnp.zeros((3, 3, 8, total), f32)], axis=2
    )
    table = table.reshape(9, ROWS, tiles, TILE).transpose(0, 2, 1, 3).reshape(9 * tiles, ROWS, TILE)
    near = (ax >= 0) & (ax < CX + 2 * REACH) & (ay >= -REACH) & (ay < CY + REACH)
    bucket = (ax.astype(jnp.int32) // BX).reshape(9 * tiles, TILE)
    near = near.reshape(9 * tiles, TILE)
    lo = jnp.min(jnp.where(near, bucket, 99), axis=1)
    hi = jnp.max(jnp.where(near, bucket, -1), axis=1)

    raw = kernel_taps()
    scale = 1.0 / jnp.sum(raw)
    unit = raw * scale
    rows = jnp.arange(ROWS)[:, None]
    lanes = jnp.arange(384)[None, :] // 128
    pick = jnp.where(lanes == 0, jnp.where(rows == 6, 16.0, jnp.where(rows == 7, 1.0, 0.0)), 0.0)
    pick = jnp.where((lanes == 1) & (rows == 5), 1.0, pick)
    pick = jnp.where((lanes == 2) & (rows == 4), 1.0, pick).astype(bf16)

    density = spread_call(lo, hi, raw, table, pick[:, :128], field)
    partial = sample_call(lo, hi, unit, table, pick, background, density, scale[None])
    partial = partial[:, :3].reshape(3, 3, tiles, 3, TILE).transpose(0, 1, 3, 2, 4).reshape(3, 3, 3, total)
    mine = partial[1] + ring(partial[2], 1) + ring(partial[0], -1)
    own = mine[1] + line(mine[2], 1) + line(mine[0], -1)
    _, *vel = lax.sort((order, own[0], own[1], own[2]), num_keys=1)
    velocity = jnp.stack([v.reshape(9, cap) for v in vel], axis=1)[None]
    return density, velocity


def solution(mesh):
    return jax.shard_map(
        on_device,
        mesh=mesh,
        in_specs=(
            P(("stream", "span"), None, None, None),
            P(("stream", "span"), None, None),
            P(("stream", "span"), None),
            P(),
            P(),
        ),
        out_specs=(P(None, "stream", "span", None), P(("stream", "span"), None, None, None)),
        check_vma=False,
    )
```

```python
import functools

import jax
import jax.numpy as jnp
from jax import lax
from jax.experimental import pallas as pl
from jax.experimental.pallas import tpu as pltpu
from jax.sharding import PartitionSpec as P

CX = 64
CY = 16
NZ = 512
REACH = 6
TILE = 128
BX = 8
XO = 8
XROWS = 84
BP = BX * CY

spread_width = 12.5


def kernel_taps():
    offsets = jnp.arange(-6, 7).astype(jnp.float32)
    return jnp.exp(-offsets * offsets / spread_width)


def gauss(d):
    return jnp.where(jnp.abs(d) < REACH + 0.5, jnp.exp(d * d * (-1.0 / spread_width)), 0.0)


def hi_lo(v):
    hi = v.astype(jnp.bfloat16)
    lo = (v - hi.astype(jnp.float32)).astype(jnp.bfloat16)
    return hi, lo


def columns(xt, pick):
    return lax.dot_general(
        xt.astype(jnp.bfloat16), pick, (((0,), (0,)), ((), ())), preferred_element_type=jnp.float32
    )


def x_filtered(load, taps, count):
    outs = []
    ins = [load(i) for i in range(count + 12)]
    for o in range(count):
        total = taps[6] * ins[o + 6]
        for k in range(1, 7):
            total = total + taps[6 + k] * (ins[o + 6 - k] + ins[o + 6 + k])
        outs.append(total)
    return outs


def tile_codes(list_ref, tab_ref, k):
    code = list_ref[k + 1]
    i = code >> 14
    per = list_ref[0]
    n = jnp.where(per == 0, 4, lax.div(i, jnp.maximum(per, 1)))
    return i, n, (code >> 7) & 127, code & 127


def framed(tab_ref, i, n):
    xt = tab_ref[i].astype(jnp.float32)
    row, col = lax.div(n, 3), lax.rem(n, 3)
    sx = ((row - 1) * CX + REACH).astype(jnp.float32)
    sy = ((col - 1) * CY).astype(jnp.float32)
    return xt, sx, sy


def accumulate(count_ref, list_ref, tab_ref, pick_ref, acc, amat, zmat):
    def tile(k, _):
        i, n, first, last = tile_codes(list_ref, tab_ref, k)
        xt, sx, sy = framed(tab_ref, i, n)
        zrep = columns(xt, pick_ref[...])
        lane = lax.broadcasted_iota(jnp.int32, (TILE, 128), 1).astype(jnp.float32)
        for q in range(NZ // 128):
            hit = jnp.where(lane + (128.0 * q) == zrep, 1.0, 0.0).astype(jnp.bfloat16)
            cols = slice(128 * q, 128 * (q + 1))
            zmat[0:TILE, cols] = hit
            zmat[TILE : 2 * TILE, cols] = hit
        ypl = lax.broadcasted_iota(jnp.int32, (CY, TILE), 0).astype(jnp.float32)
        gy = gauss(ypl - (xt[5:6, :] + sy))
        xrow = xt[4:5, :] + sx
        parts = [hi_lo(gy * xt[c : c + 1, :]) for c in range(4)]

        def window(w, _):
            x0 = first + w * BX
            for xx in range(BX):
                at = (x0 + xx).astype(jnp.float32)
                m = jnp.where(xrow == at, 1.0, 0.0)
                m = jnp.broadcast_to(m, (CY, TILE)).astype(jnp.bfloat16)
                for c in range(4):
                    rows = slice((xx * 4 + c) * CY, (xx * 4 + c + 1) * CY)
                    amat[rows, 0:TILE] = parts[c][0] * m
                    amat[rows, TILE : 2 * TILE] = parts[c][1] * m
            part = jnp.dot(amat[...], zmat[...], preferred_element_type=jnp.float32)
            acc[pl.ds(x0, BX)] += part.reshape(BX, 4 * CY, NZ)
            return 0

        lax.fori_loop(0, (last - first) // BX + 1, window, 0)
        return 0

    lax.fori_loop(0, count_ref[0], tile, 0)


def spread_own_kernel(count_ref, list_ref, tab_ref, pick_ref, out_ref, acc, amat, zmat, sem):
    def clear(i, _):
        acc[i] = jnp.zeros(acc.shape[1:], jnp.float32)
        return 0

    lax.fori_loop(0, XROWS, clear, 0)
    accumulate(count_ref, list_ref, tab_ref, pick_ref, acc, amat, zmat)
    copy = pltpu.make_async_copy(acc, out_ref, sem)
    copy.start()
    copy.wait()


def spread_kernel(
    count_ref, list_ref, taps_ref, tab_ref, pick_ref, field_ref, band_ref, old_ref, out_ref, acc, amat, zmat, wide, sem
):
    step = pl.program_id(0)

    @pl.when(step == 0)
    def _():
        copy = pltpu.make_async_copy(old_ref, acc, sem)
        copy.start()
        copy.wait()
        accumulate(count_ref, list_ref, tab_ref, pick_ref, acc, amat, zmat)

    @pl.when(step > 0)
    def _():
        base = (step - 1) * XO
        taps = [taps_ref[k] for k in range(13)]

        def chunk(j, _):
            cols = pl.ds(pl.multiple_of(j * 128, 128), 128)
            for c in range(4):
                outs = x_filtered(lambda i: acc[base + i, c * CY : (c + 1) * CY, cols], taps, XO)
                for o in range(XO):
                    hi, lo = hi_lo(outs[o])
                    rows = slice((c * XO + o) * CY, (c * XO + o + 1) * CY)
                    wide[0, rows, cols] = hi
                    wide[1, rows, cols] = lo
            return 0

        lax.fori_loop(0, NZ // 128, chunk, 0)
        hi, lo = wide[0], wide[1]
        full = jnp.concatenate([hi, hi, lo], axis=1)
        dens = jnp.dot(full, band_ref[...], preferred_element_type=jnp.float32)
        dens = dens.reshape(4, XO, CY, NZ)
        out_ref[3] = dens[3]
        for c in range(3):
            out_ref[c] = dens[c] + dens[3] * field_ref[c : c + 1, :][None]


def sampled(count_ref, list_ref, scale_ref, tab_ref, pick_ref, fmat, out_ref, gathered):
    scale = scale_ref[0]
    out_ref[...] = jnp.zeros(out_ref.shape, jnp.float32)

    def tile(k, _):
        i, n, first, last = tile_codes(list_ref, tab_ref, k)
        xt, sx, sy = framed(tab_ref, i, n)
        cols = columns(xt, pick_ref[...])
        xrep, yrep, zrep = (cols[:, 128 * k : 128 * (k + 1)] for k in (2, 1, 0))
        lane_i = lax.broadcasted_iota(jnp.int32, (TILE, 128), 1)
        lane = lane_i.astype(jnp.float32)
        xpl = (lane_i // CY).astype(jnp.float32)
        ypl = (lane_i % CY).astype(jnp.float32)
        wy = gauss(ypl - (yrep + sy)) * scale
        xoff = xrep - xpl

        def part(w):
            x0 = first + w * BX
            a = jnp.where(xoff == x0.astype(jnp.float32) - sx, wy, 0.0)
            full = jnp.concatenate(hi_lo(a), axis=1)
            f = fmat[pl.ds(x0, BX)].reshape(BP, 3 * NZ)
            return jnp.dot(full, jnp.concatenate([f, f], axis=0), preferred_element_type=jnp.float32)

        gathered[...] = part(jnp.int32(0))

        def window(w, _):
            gathered[...] += part(w)
            return 0

        lax.fori_loop(1, (last - first) // BX + 1, window, 0)
        sums = [None] * 3
        for q in range(NZ // 128):
            wz = gauss(lane + (128.0 * q) - zrep) * scale
            for c in range(3):
                t = gathered[:, c * NZ + 128 * q : c * NZ + 128 * (q + 1)] * wz
                sums[c] = t if sums[c] is None else sums[c] + t
        ones = jnp.ones((8, 256), jnp.bfloat16)
        for c in range(3):
            both = jnp.concatenate(hi_lo(sums[c]), axis=1)
            row = lax.dot_general(ones, both, (((1,), (1,)), ((), ())), preferred_element_type=jnp.float32)
            out_ref[i, c : c + 1, :] = row[0:1, :]
        return 0

    lax.fori_loop(0, count_ref[0], tile, 0)


def sample_kernel(
    count_ref,
    list_ref,
    taps_ref,
    scale_ref,
    tab_ref,
    pick_ref,
    ground_ref,
    dens_ref,
    out_ref,
    fmat,
    flow,
    gathered,
):
    step = pl.program_id(0)
    last_step = pl.num_programs(0) - 1

    @pl.when(step == 0)
    def _():
        def clear(i, _):
            flow[:, i] = jnp.zeros((3, CY, NZ), jnp.float32)
            flow[:, 12 + CX + i] = jnp.zeros((3, CY, NZ), jnp.float32)
            return 0

        lax.fori_loop(0, 12, clear, 0)
        for i in range(12 + CX + 12, flow.shape[1]):
            flow[:, i] = jnp.zeros((3, CY, NZ), jnp.float32)

    @pl.when(step < last_step)
    def _():
        for c in range(3):
            g = ground_ref[c : c + 1, :]
            for i in range(XO):
                flow[c, 12 + step * XO + i] = dens_ref[c, i] + g

    @pl.when(step == last_step)
    def _():
        taps = [taps_ref[k] for k in range(13)]

        def block(b, _):
            for c in range(3):

                def chunk(j, _, c=c):
                    cols = pl.ds(pl.multiple_of(j * 128, 128), 128)
                    dest = pl.ds(pl.multiple_of(c * NZ + j * 128, 128), 128)
                    outs = x_filtered(lambda i: flow[c, b * 4 + i, :, cols], taps, 4)
                    for o in range(4):
                        fmat[b * 4 + o, :, dest] = outs[o].astype(jnp.bfloat16)
                    return 0

                lax.fori_loop(0, NZ // 128, chunk, 0)
            return 0

        lax.fori_loop(0, XROWS // 4, block, 0)
        sampled(count_ref, list_ref, scale_ref, tab_ref, pick_ref, fmat, out_ref, gathered)


def sample_own_kernel(count_ref, list_ref, scale_ref, tab_ref, pick_ref, fmat, out_ref, gathered):
    sampled(count_ref, list_ref, scale_ref, tab_ref, pick_ref, fmat, out_ref, gathered)


def smem():
    return pl.BlockSpec(memory_space=pltpu.SMEM)


def whole(shape):
    return pl.BlockSpec(shape, lambda i: (0,) * len(shape))


PARAMS = pltpu.CompilerParams(vmem_limit_bytes=56 << 20)


def spread_own_call(listing, table, pick):
    acc = (XROWS, 4 * CY, NZ)
    return pl.pallas_call(
        spread_own_kernel,
        grid=(1,),
        in_specs=[smem(), smem(), whole(table.shape), whole(pick.shape)],
        out_specs=pl.BlockSpec(memory_space=pl.ANY),
        out_shape=jax.ShapeDtypeStruct(acc, jnp.float32),
        scratch_shapes=[
            pltpu.VMEM(acc, jnp.float32),
            pltpu.VMEM((4 * BP, 2 * TILE), jnp.bfloat16),
            pltpu.VMEM((2 * TILE, NZ), jnp.bfloat16),
            pltpu.SemaphoreType.DMA,
        ],
        compiler_params=PARAMS,
        cost_estimate=pl.CostEstimate(flops=10**10, transcendentals=0, bytes_accessed=3 * 10**7),
        name="spread_own",
    )(*listing, table, pick)


def spread_call(listing, taps, table, pick, field, band, old):
    steps = CX // XO
    return pl.pallas_call(
        spread_kernel,
        grid=(steps + 1,),
        in_specs=[smem(), smem(), smem(), whole(table.shape), whole(pick.shape), whole(field.shape), whole(band.shape)]
        + [pl.BlockSpec(memory_space=pl.ANY)],
        out_specs=pl.BlockSpec((4, XO, CY, NZ), lambda i: (0, jnp.maximum(i - 1, 0), 0, 0)),
        out_shape=jax.ShapeDtypeStruct((4, CX, CY, NZ), jnp.float32),
        scratch_shapes=[
            pltpu.VMEM(old.shape, jnp.float32),
            pltpu.VMEM((4 * BP, 2 * TILE), jnp.bfloat16),
            pltpu.VMEM((2 * TILE, NZ), jnp.bfloat16),
            pltpu.VMEM((2, 4 * XO * CY, NZ), jnp.bfloat16),
            pltpu.SemaphoreType.DMA,
        ],
        compiler_params=PARAMS,
        cost_estimate=pl.CostEstimate(flops=2 * 10**10, transcendentals=0, bytes_accessed=3 * 10**7),
        name="spread_rest",
    )(*listing, taps, table, pick, field, band, old)


def sample_call(listing, taps, scale, table, pick, ground, density):
    n = table.shape[0]
    steps = CX // XO
    fshape = (XROWS, CY, 3 * NZ)
    return pl.pallas_call(
        sample_kernel,
        grid=(steps + 1,),
        in_specs=[
            smem(),
            smem(),
            smem(),
            smem(),
            whole(table.shape),
            whole(pick.shape),
            whole(ground.shape),
            pl.BlockSpec((3, XO, CY, NZ), lambda i: (0, jnp.minimum(i, steps - 1), 0, 0)),
        ],
        out_specs=[whole((n, 8, TILE)), whole(fshape)],
        out_shape=[jax.ShapeDtypeStruct((n, 8, TILE), jnp.float32), jax.ShapeDtypeStruct(fshape, jnp.bfloat16)],
        scratch_shapes=[
            pltpu.VMEM((3, XROWS + 12, CY, NZ), jnp.float32),
            pltpu.VMEM((TILE, 3 * NZ), jnp.float32),
        ],
        compiler_params=PARAMS,
        cost_estimate=pl.CostEstimate(flops=2 * 10**10, transcendentals=0, bytes_accessed=3 * 10**7),
        name="sample_rest",
    )(*listing, taps, scale, table, pick, ground, density)


def sample_own_call(listing, scale, table, pick, fmat):
    n = table.shape[0]
    return pl.pallas_call(
        sample_own_kernel,
        grid=(1,),
        in_specs=[smem(), smem(), smem(), whole(table.shape), whole(pick.shape), whole(fmat.shape)],
        out_specs=whole((n, 8, TILE)),
        out_shape=jax.ShapeDtypeStruct((n, 8, TILE), jnp.float32),
        scratch_shapes=[pltpu.VMEM((TILE, 3 * NZ), jnp.float32)],
        compiler_params=PARAMS,
        cost_estimate=pl.CostEstimate(flops=10**10, transcendentals=0, bytes_accessed=3 * 10**7),
        name="sample_own",
    )(*listing, scale, table, pick, fmat)


def listed(x, y, exists, sx, sy, per):
    ax, ay = x + sx, y + sy
    near = (ax >= 0) & (ax < CX + 2 * REACH) & (ay >= -REACH) & (ay < CY + REACH) & exists
    lo = jnp.min(jnp.where(near, ax, 127), axis=-1).reshape(-1)
    hi = jnp.max(jnp.where(near, ax, -1), axis=-1).reshape(-1)
    active = hi >= 0
    at = jnp.arange(lo.shape[0], dtype=jnp.int32)
    pos = jnp.sum((at[None, :] < at[:, None]) & active[None, :], axis=1, dtype=jnp.int32)
    code = ((at * 128) + lo) * 128 + hi
    rows = jnp.sum(jnp.where((pos[None, :] == at[:, None]) & active[None, :], code[None, :], 0), axis=1)
    count = jnp.sum(active, dtype=jnp.int32)
    return count[None], jnp.concatenate([jnp.array([per], jnp.int32), rows])


def ring(value, steps):
    count = lax.axis_size("stream")
    return lax.ppermute(value, "stream", [(i, (i + steps) % count) for i in range(count)])


def line(value, steps):
    count = lax.axis_size("span")
    first, last = max(0, -steps), min(count, count - steps)
    return lax.ppermute(value, "span", [(i, i + steps) for i in range(first, last)])


def on_device(records, cells, counts, background, field):
    cap = records.shape[3]
    total = 9 * cap
    tiles = total // TILE
    bf16, f32 = jnp.bfloat16, jnp.float32
    slots = jnp.arange(cap, dtype=jnp.int32)
    live = slots[None, :] < counts[0][:, None]
    cell = cells[0]
    z = cell % NZ
    x = jnp.where(live, cell // (CY * NZ), 255)
    y = (cell // NZ) % CY
    places = jnp.stack([x, y, z // 16, z % 16], axis=1).astype(bf16)
    outgoing = jnp.concatenate([records[0], places], axis=1).reshape(3, 3, 8, cap)
    dead = jnp.zeros((8,), bf16).at[4].set(255)[:, None]
    outgoing = jnp.stack([ring(outgoing[0], -1), outgoing[1], ring(outgoing[2], 1)])
    me = lax.axis_index("span")
    spans = lax.axis_size("span")
    has_low, has_high = me > 0, me < spans - 1
    from_high = jnp.where(has_high, line(outgoing[:, 0], -1), dead)
    from_low = jnp.where(has_low, line(outgoing[:, 2], 1), dead)
    inbound = jnp.stack([from_high, outgoing[:, 1], from_low], axis=1)
    inbound = inbound.transpose(2, 0, 1, 3).reshape(8, total)

    gi = inbound[4:].astype(jnp.int32)
    gx, gy, gz = gi[0], gi[1], gi[2] * 16 + gi[3]
    klass = (gy >= REACH).astype(jnp.int32) + (gy >= CY - REACH)
    klass = jnp.where(gx > 200, 3, klass)
    kx = jnp.where(klass == 1, CX - 1 - gx, gx)
    key = ((klass * 256 + kx) * CY + gy) * NZ + gz
    order = jnp.arange(total, dtype=jnp.int32)
    key, order, *vals = lax.sort((key, order) + tuple(inbound[c].astype(f32) for c in range(4)), num_keys=1)
    sz = key % NZ
    sy = key // NZ % CY
    sx = key // (CY * NZ) % 256
    sx = jnp.where(key // (CY * NZ * 256) == 1, CX - 1 - sx, sx)
    packed = jnp.stack(vals + [v.astype(f32) for v in (sx, sy, sz // 16, sz % 16)]).astype(bf16)
    packed = packed.reshape(8, tiles, TILE).transpose(1, 0, 2)

    low = line(packed, 1)
    high = line(packed, -1)
    three = jnp.stack([low, packed, high])
    arrays = jnp.stack([ring(three, 1), three, ring(three, -1)])
    own_list = listed(
        sx.reshape(tiles, TILE), sy.reshape(tiles, TILE), sx.reshape(tiles, TILE) < 200, REACH, 0, 0
    )
    places = arrays[:, :, :, 4:6].astype(jnp.int32)
    shift = jnp.arange(-1, 2, dtype=jnp.int32)
    exists = jnp.stack([has_low, jnp.array(True), has_high])
    exists = exists[None, :] & ~((shift[:, None] == 0) & (shift[None, :] == 0))
    rest_list = listed(
        places[:, :, :, 0],
        places[:, :, :, 1],
        exists[:, :, None, None],
        CX * shift[:, None, None, None] + REACH,
        CY * shift[None, :, None, None],
        tiles,
    )
    table = arrays.reshape(9 * tiles, 8, TILE)

    raw = kernel_taps()
    scale = 1.0 / jnp.sum(raw)
    unit = raw * scale
    rows = jnp.arange(8)[:, None]
    lanes = jnp.arange(384)[None, :] // 128
    pick = jnp.where(lanes == 0, jnp.where(rows == 6, 16.0, jnp.where(rows == 7, 1.0, 0.0)), 0.0)
    pick = jnp.where((lanes == 1) & (rows == 5), 1.0, pick)
    pick = jnp.where((lanes == 2) & (rows == 4), 1.0, pick).astype(bf16)

    zs = jnp.arange(NZ)
    exact = gauss((zs[:, None] - zs[None, :]).astype(f32))
    coarse = lax.reduce_precision(exact, 8, 7)
    band = jnp.concatenate([coarse, exact - coarse, coarse], axis=0).astype(bf16)

    half = spread_own_call(own_list, packed, pick[:, :128])
    density = spread_call(rest_list, raw, table, pick[:, :128], field, band, half)
    partial, fmat = sample_call(rest_list, unit, scale[None], table, pick, background, density)
    mine = sample_own_call(own_list, scale[None], packed, pick, fmat)[:, :3]
    partial = partial[:, :3].reshape(3, 3, tiles, 3, TILE)
    mixed = partial[1] + ring(partial[2], 1) + ring(partial[0], -1)
    own = mixed[1] + mine + line(mixed[2], 1) + line(mixed[0], -1)
    own = own.transpose(1, 0, 2).reshape(3, total)
    _, *vel = lax.sort((order, own[0], own[1], own[2]), num_keys=1)
    velocity = jnp.stack([v.reshape(9, cap) for v in vel], axis=1)[None]
    return density, velocity


def solution(mesh):
    return jax.shard_map(
        on_device,
        mesh=mesh,
        in_specs=(
            P(("stream", "span"), None, None, None),
            P(("stream", "span"), None, None),
            P(("stream", "span"), None),
            P(),
            P(),
        ),
        out_specs=(P(None, "stream", "span", None), P(("stream", "span"), None, None, None)),
        check_vma=False,
    )
```

```python
import functools

import jax
import jax.numpy as jnp
from jax import lax
from jax.experimental import pallas as pl
from jax.experimental.pallas import tpu as pltpu
from jax.sharding import PartitionSpec as P

CX = 64
CY = 16
NZ = 512
REACH = 6
TILE = 128
BX = 8
XO = 8
XROWS = 84
BUCKETS = 10
FROWS = 92
BP = BX * CY

spread_width = 12.5


def kernel_taps():
    offsets = jnp.arange(-6, 7).astype(jnp.float32)
    return jnp.exp(-offsets * offsets / spread_width)


def gauss(d):
    return jnp.where(jnp.abs(d) < REACH + 0.5, jnp.exp(d * d * (-1.0 / spread_width)), 0.0)


def hi_lo(v):
    hi = v.astype(jnp.bfloat16)
    lo = (v - hi.astype(jnp.float32)).astype(jnp.bfloat16)
    return hi, lo


def columns(xt, pick):
    return lax.dot_general(
        xt.astype(jnp.bfloat16), pick, (((0,), (0,)), ((), ())), preferred_element_type=jnp.float32
    )


def x_filtered(load, taps, count):
    outs = []
    ins = [load(i) for i in range(count + 12)]
    for o in range(count):
        total = taps[6] * ins[o + 6]
        for k in range(1, 7):
            total = total + taps[6 + k] * (ins[o + 6 - k] + ins[o + 6 + k])
        outs.append(total)
    return outs


def tile_codes(list_ref, tab_ref, k):
    code = list_ref[k + 1]
    i = code >> 14
    per = list_ref[0]
    n = jnp.where(per == 0, 4, lax.div(i, jnp.maximum(per, 1)))
    return i, n, (code >> 7) & 127, code & 127


def framed(tab_ref, i, n):
    xt = tab_ref[i].astype(jnp.float32)
    row, col = lax.div(n, 3), lax.rem(n, 3)
    sx = ((row - 1) * CX + REACH).astype(jnp.float32)
    sy = ((col - 1) * CY).astype(jnp.float32)
    return xt, sx, sy


def accumulate(bounds_ref, list_ref, tab_ref, pick_ref, acc, amat, zmat):
    def tile(k, _):
        i, n, first, last = tile_codes(list_ref, tab_ref, k)
        xt, sx, sy = framed(tab_ref, i, n)
        zrep = columns(xt, pick_ref[:, 0:128])
        lane = lax.broadcasted_iota(jnp.int32, (TILE, 128), 1).astype(jnp.float32)
        for q in range(NZ // 128):
            hit = jnp.where(lane + (128.0 * q) == zrep, 1.0, 0.0).astype(jnp.bfloat16)
            cols = slice(128 * q, 128 * (q + 1))
            zmat[0:TILE, cols] = hit
            zmat[TILE : 2 * TILE, cols] = hit
        ypl = lax.broadcasted_iota(jnp.int32, (CY, TILE), 0).astype(jnp.float32)
        gy = gauss(ypl - (xt[5:6, :] + sy))
        xrow = xt[4:5, :] + sx
        parts = [hi_lo(gy * xt[c : c + 1, :]) for c in range(4)]

        def window(w, _):
            x0 = first + w * BX
            for xx in range(BX):
                at = (x0 + xx).astype(jnp.float32)
                m = jnp.where(xrow == at, 1.0, 0.0)
                m = jnp.broadcast_to(m, (CY, TILE)).astype(jnp.bfloat16)
                for c in range(4):
                    rows = slice((xx * 4 + c) * CY, (xx * 4 + c + 1) * CY)
                    amat[rows, 0:TILE] = parts[c][0] * m
                    amat[rows, TILE : 2 * TILE] = parts[c][1] * m
            part = jnp.dot(amat[...], zmat[...], preferred_element_type=jnp.float32)
            acc[pl.ds(x0, BX)] += part.reshape(BX, 4 * CY, NZ)
            return 0

        lax.fori_loop(0, (last - first) // BX + 1, window, 0)
        return 0

    lax.fori_loop(bounds_ref[0], bounds_ref[1], tile, 0)


def spread_own_kernel(bounds_ref, list_ref, tab_ref, pick_ref, out_ref, acc, amat, zmat, sem):
    def clear(i, _):
        acc[i] = jnp.zeros(acc.shape[1:], jnp.float32)
        return 0

    lax.fori_loop(0, XROWS, clear, 0)
    accumulate(bounds_ref, list_ref, tab_ref, pick_ref, acc, amat, zmat)
    copy = pltpu.make_async_copy(acc, out_ref, sem)
    copy.start()
    copy.wait()


def sampled(bounds_ref, list_ref, scale_ref, tab_ref, pick_ref, fmat, out_ref, gathered):
    scale = scale_ref[0]
    out_ref[...] = jnp.zeros(out_ref.shape, jnp.float32)

    def tile(k, _):
        i, n, first, last = tile_codes(list_ref, tab_ref, k)
        xt, sx, sy = framed(tab_ref, i, n)
        cols = columns(xt, pick_ref[...])
        xrep, yrep, zrep = (cols[:, 128 * k : 128 * (k + 1)] for k in (2, 1, 0))
        lane_i = lax.broadcasted_iota(jnp.int32, (TILE, 128), 1)
        lane = lane_i.astype(jnp.float32)
        xpl = (lane_i // CY).astype(jnp.float32)
        ypl = (lane_i % CY).astype(jnp.float32)
        wy = gauss(ypl - (yrep + sy)) * scale
        xoff = xrep - xpl

        def part(x0, blocks):
            lhs, rhs = [], []
            for k in range(blocks):
                a = jnp.where(xoff == (x0 + k * BX).astype(jnp.float32) - sx, wy, 0.0)
                lhs.extend(hi_lo(a))
                f = fmat[pl.ds(x0 + k * BX, BX)].reshape(BP, 3 * NZ)
                rhs.extend([f, f])
            return jnp.dot(
                jnp.concatenate(lhs, axis=1), jnp.concatenate(rhs, axis=0), preferred_element_type=jnp.float32
            )

        @pl.when(last - first < BX)
        def _():
            gathered[...] = part(first, 1)

        @pl.when(last - first >= BX)
        def _():
            gathered[...] = part(first, 2)

            def window(w, _):
                gathered[...] += part(first + w * (2 * BX), 2)
                return 0

            lax.fori_loop(1, (last - first) // (2 * BX) + 1, window, 0)

        sums = [None] * 3
        for q in range(NZ // 128):
            wz = gauss(lane + (128.0 * q) - zrep) * scale
            for c in range(3):
                t = gathered[:, c * NZ + 128 * q : c * NZ + 128 * (q + 1)] * wz
                sums[c] = t if sums[c] is None else sums[c] + t
        for c in range(3):
            out_ref[i, c : c + 1, :] = jnp.sum(sums[c].T, axis=0, keepdims=True)
        return 0

    lax.fori_loop(bounds_ref[0], bounds_ref[1], tile, 0)


def main_kernel(
    bounds_ref,
    list_ref,
    raw_ref,
    unit_ref,
    scale_ref,
    tab_ref,
    pick_ref,
    field_ref,
    ground_ref,
    band_ref,
    old_ref,
    dens_ref,
    out_ref,
    fmat,
    acc,
    amat,
    zmat,
    wide_a,
    wide_b,
    flow,
    gathered,
    sem,
):
    step = pl.program_id(0)
    steps = CX // XO
    raw = [raw_ref[k] for k in range(13)]

    def filtered(b, wide):
        base = b * XO
        for q in range(NZ // 128):
            cols = slice(q * 128, (q + 1) * 128)
            for c in range(4):
                outs = x_filtered(lambda i: acc[base + i, c * CY : (c + 1) * CY, cols], raw, XO)
                for o in range(XO):
                    hi, lo = hi_lo(outs[o])
                    rows = slice((c * XO + o) * CY, (c * XO + o + 1) * CY)
                    wide[0, rows, cols] = hi
                    wide[1, rows, cols] = lo

    def finish(b, wide):
        hi, lo = wide[0], wide[1]
        full = jnp.concatenate([hi, hi, lo], axis=1)
        dens = jnp.dot(full, band_ref[...], preferred_element_type=jnp.float32)
        dens = dens.reshape(4, XO, CY, NZ)
        dens_ref[3] = dens[3]
        for c in range(3):
            d = dens[c] + dens[3] * field_ref[c : c + 1, :][None]
            dens_ref[c] = d
            flow[c, pl.ds(12 + b * XO, XO)] = d + ground_ref[c : c + 1, :][None]

    @pl.when(step == 0)
    def _():
        copy = pltpu.make_async_copy(old_ref, acc, sem)
        copy.start()

        def clear(i, _):
            flow[:, i] = jnp.zeros((3, CY, NZ), jnp.float32)
            flow[:, 12 + CX + i] = jnp.zeros((3, CY, NZ), jnp.float32)
            return 0

        lax.fori_loop(0, 16, clear, 0)
        for i in range(BUCKETS * BX, FROWS):
            fmat[i] = jnp.zeros(fmat.shape[1:], jnp.bfloat16)
        copy.wait()
        accumulate(bounds_ref, list_ref, tab_ref, pick_ref, acc, amat, zmat)
        filtered(0, wide_a)

    for parity, now, later in ((1, wide_a, wide_b), (0, wide_b, wide_a)):

        @pl.when((step > 0) & (step <= steps) & (step % 2 == parity))
        def _(now=now, later=later):
            finish(step - 1, now)
            filtered(jnp.minimum(step, steps - 1), later)

    @pl.when(step > steps)
    def _():
        taps = [unit_ref[k] for k in range(13)]

        def block(b, _):
            for c in range(3):

                def chunk(j, _, c=c):
                    cols = pl.ds(pl.multiple_of(j * 128, 128), 128)
                    dest = pl.ds(pl.multiple_of(c * NZ + j * 128, 128), 128)
                    outs = x_filtered(lambda i: flow[c, b * BX + i, :, cols], taps, BX)
                    for o in range(BX):
                        fmat[b * BX + o, :, dest] = outs[o].astype(jnp.bfloat16)
                    return 0

                lax.fori_loop(0, NZ // 128, chunk, 0)
            return 0

        lax.fori_loop(0, BUCKETS, block, 0)
        sampled(bounds_ref, list_ref, scale_ref, tab_ref, pick_ref, fmat, out_ref, gathered)


def sample_own_kernel(bounds_ref, list_ref, scale_ref, tab_ref, pick_ref, fmat, out_ref, gathered):
    sampled(bounds_ref, list_ref, scale_ref, tab_ref, pick_ref, fmat, out_ref, gathered)


def smem():
    return pl.BlockSpec(memory_space=pltpu.SMEM)


def whole(shape):
    return pl.BlockSpec(shape, lambda i: (0,) * len(shape))


PARAMS = pltpu.CompilerParams(vmem_limit_bytes=56 << 20)


def spread_own_call(listing, table, pick):
    acc = (XROWS, 4 * CY, NZ)
    return pl.pallas_call(
        spread_own_kernel,
        grid=(1,),
        in_specs=[smem(), smem(), whole(table.shape), whole(pick.shape)],
        out_specs=pl.BlockSpec(memory_space=pl.ANY),
        out_shape=jax.ShapeDtypeStruct(acc, jnp.float32),
        scratch_shapes=[
            pltpu.VMEM(acc, jnp.float32),
            pltpu.VMEM((4 * BP, 2 * TILE), jnp.bfloat16),
            pltpu.VMEM((2 * TILE, NZ), jnp.bfloat16),
            pltpu.SemaphoreType.DMA,
        ],
        compiler_params=PARAMS,
        cost_estimate=pl.CostEstimate(flops=10**10, transcendentals=0, bytes_accessed=3 * 10**7),
        name="spread_own",
    )(*listing, table, pick)


def main_call(listing, raw, unit, scale, table, pick, field, ground, band, old):
    steps = CX // XO
    n = table.shape[0]
    fshape = (FROWS, CY, 3 * NZ)
    return pl.pallas_call(
        main_kernel,
        grid=(steps + 2,),
        in_specs=[smem()] * 5
        + [whole(v.shape) for v in (table, pick, field, ground, band)]
        + [pl.BlockSpec(memory_space=pl.ANY)],
        out_specs=[
            pl.BlockSpec((4, XO, CY, NZ), lambda i: (0, jnp.clip(i - 1, 0, steps - 1), 0, 0)),
            whole((n, 8, TILE)),
            whole(fshape),
        ],
        out_shape=[
            jax.ShapeDtypeStruct((4, CX, CY, NZ), jnp.float32),
            jax.ShapeDtypeStruct((n, 8, TILE), jnp.float32),
            jax.ShapeDtypeStruct(fshape, jnp.bfloat16),
        ],
        scratch_shapes=[
            pltpu.VMEM(old.shape, jnp.float32),
            pltpu.VMEM((4 * BP, 2 * TILE), jnp.bfloat16),
            pltpu.VMEM((2 * TILE, NZ), jnp.bfloat16),
            pltpu.VMEM((2, 4 * XO * CY, NZ), jnp.bfloat16),
            pltpu.VMEM((2, 4 * XO * CY, NZ), jnp.bfloat16),
            pltpu.VMEM((3, BUCKETS * BX + 12, CY, NZ), jnp.float32),
            pltpu.VMEM((TILE, 3 * NZ), jnp.float32),
            pltpu.SemaphoreType.DMA,
        ],
        compiler_params=PARAMS,
        cost_estimate=pl.CostEstimate(flops=4 * 10**10, transcendentals=0, bytes_accessed=6 * 10**7),
        name="main",
    )(*listing, raw, unit, scale, table, pick, field, ground, band, old)


def sample_own_call(listing, scale, table, pick, fmat):
    n = table.shape[0]
    return pl.pallas_call(
        sample_own_kernel,
        grid=(1,),
        in_specs=[smem(), smem(), smem(), whole(table.shape), whole(pick.shape), whole(fmat.shape)],
        out_specs=whole((n, 8, TILE)),
        out_shape=jax.ShapeDtypeStruct((n, 8, TILE), jnp.float32),
        scratch_shapes=[pltpu.VMEM((TILE, 3 * NZ), jnp.float32)],
        compiler_params=PARAMS,
        cost_estimate=pl.CostEstimate(flops=10**10, transcendentals=0, bytes_accessed=3 * 10**7),
        name="sample_own",
    )(*listing, scale, table, pick, fmat)


def listed(x, y, exists, sx, sy, per):
    ax, ay = x + sx, y + sy
    near = (ax >= 0) & (ax < CX + 2 * REACH) & (ay >= -REACH) & (ay < CY + REACH) & exists
    lo = jnp.min(jnp.where(near, ax, 127), axis=-1).reshape(-1)
    hi = jnp.max(jnp.where(near, ax, -1), axis=-1).reshape(-1)
    active = hi >= 0
    at = jnp.arange(lo.shape[0], dtype=jnp.int32)
    pos = jnp.sum((at[None, :] < at[:, None]) & active[None, :], axis=1, dtype=jnp.int32)
    code = ((at * 128) + lo) * 128 + hi
    rows = jnp.sum(jnp.where((pos[None, :] == at[:, None]) & active[None, :], code[None, :], 0), axis=1)
    count = jnp.sum(active, dtype=jnp.int32)
    return jnp.stack([jnp.zeros((), jnp.int32), count]), jnp.concatenate([jnp.array([per], jnp.int32), rows])


def ring(value, steps):
    count = lax.axis_size("stream")
    return lax.ppermute(value, "stream", [(i, (i + steps) % count) for i in range(count)])


def line(value, steps):
    count = lax.axis_size("span")
    first, last = max(0, -steps), min(count, count - steps)
    return lax.ppermute(value, "span", [(i, i + steps) for i in range(first, last)])


def on_device(records, cells, counts, background, field):
    cap = records.shape[3]
    total = 9 * cap
    tiles = total // TILE
    bf16, f32 = jnp.bfloat16, jnp.float32
    slots = jnp.arange(cap, dtype=jnp.int32)
    live = slots[None, :] < counts[0][:, None]
    cell = cells[0]
    z = cell % NZ
    x = jnp.where(live, cell // (CY * NZ), 255)
    y = (cell // NZ) % CY
    places = jnp.stack([x, y, z // 16, z % 16], axis=1).astype(bf16)
    outgoing = jnp.concatenate([records[0], places], axis=1).reshape(3, 3, 8, cap)
    dead = jnp.zeros((8,), bf16).at[4].set(255)[:, None]
    outgoing = jnp.stack([ring(outgoing[0], -1), outgoing[1], ring(outgoing[2], 1)])
    me = lax.axis_index("span")
    spans = lax.axis_size("span")
    has_low, has_high = me > 0, me < spans - 1
    from_high = jnp.where(has_high, line(outgoing[:, 0], -1), dead)
    from_low = jnp.where(has_low, line(outgoing[:, 2], 1), dead)
    inbound = jnp.stack([from_high, outgoing[:, 1], from_low], axis=1)
    inbound = inbound.transpose(2, 0, 1, 3).reshape(8, total)

    gi = inbound[4:].astype(jnp.int32)
    gx, gy, gz = gi[0], gi[1], gi[2] * 16 + gi[3]
    klass = (gy >= REACH).astype(jnp.int32) + (gy >= CY - REACH)
    klass = jnp.where(gx > 200, 3, klass)
    kx = jnp.where(klass == 1, CX - 1 - gx, gx)
    key = ((klass * 256 + kx) * CY + gy) * NZ + gz
    order = jnp.arange(total, dtype=jnp.int32)
    key, order, *vals = lax.sort((key, order) + tuple(inbound[c].astype(f32) for c in range(4)), num_keys=1)
    sz = key % NZ
    sy = key // NZ % CY
    sx = key // (CY * NZ) % 256
    sx = jnp.where(key // (CY * NZ * 256) == 1, CX - 1 - sx, sx)
    packed = jnp.stack(vals + [v.astype(f32) for v in (sx, sy, sz // 16, sz % 16)]).astype(bf16)
    packed = packed.reshape(8, tiles, TILE).transpose(1, 0, 2)

    low = line(packed, 1)
    high = line(packed, -1)
    three = jnp.stack([low, packed, high])
    arrays = jnp.stack([ring(three, 1), three, ring(three, -1)])
    own_list = listed(
        sx.reshape(tiles, TILE), sy.reshape(tiles, TILE), sx.reshape(tiles, TILE) < 200, REACH, 0, 0
    )
    places = arrays[:, :, :, 4:6].astype(jnp.int32)
    shift = jnp.arange(-1, 2, dtype=jnp.int32)
    exists = jnp.stack([has_low, jnp.array(True), has_high])
    exists = exists[None, :] & ~((shift[:, None] == 0) & (shift[None, :] == 0))
    rest_list = listed(
        places[:, :, :, 0],
        places[:, :, :, 1],
        exists[:, :, None, None],
        CX * shift[:, None, None, None] + REACH,
        CY * shift[None, :, None, None],
        tiles,
    )
    table = arrays.reshape(9 * tiles, 8, TILE)

    raw = kernel_taps()
    scale = 1.0 / jnp.sum(raw)
    unit = raw * scale
    rows = jnp.arange(8)[:, None]
    lanes = jnp.arange(384)[None, :] // 128
    pick = jnp.where(lanes == 0, jnp.where(rows == 6, 16.0, jnp.where(rows == 7, 1.0, 0.0)), 0.0)
    pick = jnp.where((lanes == 1) & (rows == 5), 1.0, pick)
    pick = jnp.where((lanes == 2) & (rows == 4), 1.0, pick).astype(bf16)

    zs = jnp.arange(NZ)
    exact = gauss((zs[:, None] - zs[None, :]).astype(f32))
    coarse = lax.reduce_precision(exact, 8, 7)
    band = jnp.concatenate([coarse, exact - coarse, coarse], axis=0).astype(bf16)

    half = spread_own_call(own_list, packed, pick)
    density, partial, fmat = main_call(
        rest_list, raw, unit, scale[None], table, pick, field, background, band, half
    )
    bounds, codes = own_list
    middle = (bounds[1] + 1) // 2
    early = sample_own_call((jnp.stack([bounds[0], middle]), codes), scale[None], packed, pick, fmat)
    partial = partial[:, :3].reshape(3, 3, tiles, 3, TILE)
    mixed = partial[1] + ring(partial[2], 1) + ring(partial[0], -1)
    mixed, rest = lax.optimization_barrier((mixed, jnp.stack([middle, bounds[1]])))
    late = sample_own_call((rest, codes), scale[None], packed, pick, fmat)
    mine = (early + late)[:, :3]
    own = mixed[1] + mine + line(mixed[2], 1) + line(mixed[0], -1)
    own = own.transpose(1, 0, 2).reshape(3, total)
    _, *vel = lax.sort((order, own[0], own[1], own[2]), num_keys=1)
    velocity = jnp.stack([v.reshape(9, cap) for v in vel], axis=1)[None]
    return density, velocity


def solution(mesh):
    return jax.shard_map(
        on_device,
        mesh=mesh,
        in_specs=(
            P(("stream", "span"), None, None, None),
            P(("stream", "span"), None, None),
            P(("stream", "span"), None),
            P(),
            P(),
        ),
        out_specs=(P(None, "stream", "span", None), P(("stream", "span"), None, None, None)),
        check_vma=False,
    )
```

```python
import jax
import jax.numpy as jnp
import numpy as np
from jax import lax
from jax.experimental import pallas as pl
from jax.experimental.pallas import tpu as pltpu
from jax.sharding import PartitionSpec as P

CX = 64
CY = 16
NZ = 512
REACH = 6
TILE = 128
BX = 8
XO = 8
XROWS = 84
BUCKETS = 10
FROWS = 92
BP = BX * CY

spread_width = 12.5


OFFSETS = np.arange(-6, 7).astype(np.float32)
RAW = np.exp(-OFFSETS * OFFSETS / np.float32(spread_width))
SCALE = np.float32(1.0) / np.sum(RAW)
UNIT = RAW * SCALE
PICK = np.zeros((8, 384), np.float32)
PICK[6, :128], PICK[7, :128], PICK[5, 128:256], PICK[4, 256:] = 16.0, 1.0, 1.0, 1.0


def gauss(d):
    return jnp.where(jnp.abs(d) < REACH + 0.5, jnp.exp(d * d * (-1.0 / spread_width)), 0.0)


def hi_lo(v):
    hi = v.astype(jnp.bfloat16)
    lo = (v - hi.astype(jnp.float32)).astype(jnp.bfloat16)
    return hi, lo


def columns(xt, pick):
    return lax.dot_general(
        xt.astype(jnp.bfloat16), pick, (((0,), (0,)), ((), ())), preferred_element_type=jnp.float32
    )


def x_filtered(load, taps, count):
    taps = [float(t) for t in taps]
    outs = []
    ins = [load(i) for i in range(count + 12)]
    for o in range(count):
        total = taps[6] * ins[o + 6]
        for k in range(1, 7):
            total = total + taps[6 + k] * (ins[o + 6 - k] + ins[o + 6 + k])
        outs.append(total)
    return outs


def tile_codes(list_ref, k):
    code = list_ref[k + 2]
    i = code >> 14
    per = list_ref[0]
    n = jnp.where(per == 0, 4, lax.div(i, jnp.maximum(per, 1)))
    return i, n, (code >> 7) & 127, code & 127


def in_pairs(list_ref, part, width, visit):
    count = list_ref[1]
    middle = (count + 1) // 2
    begin = middle if part == 2 else 0
    end = middle if part == 1 else count

    def pair(p, _):
        k = begin + 2 * p
        visit([tile_codes(list_ref, k)[:3], tile_codes(list_ref, jnp.minimum(k + 1, end - 1))[:3]], k + 1 < end)

        def leftover(t, _):
            i, n, first, last = tile_codes(list_ref, k + t)

            def window(w, _):
                visit([(i, n, first + w * width)], None)
                return 0

            lax.fori_loop(1, (last - first) // width + 1, window, 0)
            return 0

        lax.fori_loop(0, jnp.minimum(end - k, 2), leftover, 0)
        return 0

    lax.fori_loop(0, (end - begin + 1) // 2, pair, 0)


def framed(tab_ref, i, n):
    xt = tab_ref[i].astype(jnp.float32)
    row, col = lax.div(n, 3), lax.rem(n, 3)
    sx = ((row - 1) * CX + REACH).astype(jnp.float32)
    sy = ((col - 1) * CY).astype(jnp.float32)
    return xt, sx, sy


def accumulate(list_ref, tab_ref, pick_ref, acc, amats, zmats):
    def factors(i, n, x0, amat, zmat, keep):
        xt, sx, sy = framed(tab_ref, i, n)
        zrep = columns(xt, pick_ref[:, 0:128])
        lane = lax.broadcasted_iota(jnp.int32, (TILE, 128), 1).astype(jnp.float32)
        for q in range(NZ // 128):
            hit = jnp.where(lane + (128.0 * q) == zrep, 1.0, 0.0).astype(jnp.bfloat16)
            cols = slice(128 * q, 128 * (q + 1))
            zmat[0:TILE, cols] = hit
            zmat[TILE : 2 * TILE, cols] = hit
        ypl = lax.broadcasted_iota(jnp.int32, (CY, TILE), 0).astype(jnp.float32)
        gy = gauss(ypl - (xt[5:6, :] + sy))
        if keep is not None:
            gy = jnp.where(keep, gy, 0.0)
        xrow = jnp.broadcast_to(xt[4:5, :] + sx, (CY, TILE))
        parts = [hi_lo(gy * xt[c : c + 1, :]) for c in range(4)]
        for xx in range(BX):
            m = jnp.where(xrow == (x0 + xx).astype(jnp.float32), 1.0, 0.0).astype(jnp.bfloat16)
            for c in range(4):
                rows = slice((xx * 4 + c) * CY, (xx * 4 + c + 1) * CY)
                amat[rows, 0:TILE] = parts[c][0] * m
                amat[rows, TILE : 2 * TILE] = parts[c][1] * m

    def visit(entries, second):
        for j, (i, n, x0) in enumerate(entries):
            factors(i, n, x0, amats[j], zmats[j], second if j == 1 else None)
        for j, (i, n, x0) in enumerate(entries):
            part = jnp.dot(amats[j][...], zmats[j][...], preferred_element_type=jnp.float32)
            acc[pl.ds(x0, BX)] += part.reshape(BX, 4 * CY, NZ)

    in_pairs(list_ref, 0, BX, visit)


def spread_own_kernel(list_ref, tab_ref, pick_ref, acc, amat_a, amat_b, zmat_a, zmat_b):
    def clear(i, _):
        acc[i] = jnp.zeros(acc.shape[1:], jnp.float32)
        return 0

    lax.fori_loop(0, XROWS, clear, 0)
    accumulate(list_ref, tab_ref, pick_ref, acc, (amat_a, amat_b), (zmat_a, zmat_b))


def sampled(list_ref, part, tab_ref, pick_ref, fmat, out_ref):
    scale = float(SCALE)
    out_ref[...] = jnp.zeros(out_ref.shape, jnp.float32)

    def contribution(i, n, x0):
        xt, sx, sy = framed(tab_ref, i, n)
        cols = columns(xt, pick_ref[...])
        xrep, yrep, zrep = (cols[:, 128 * k : 128 * (k + 1)] for k in (2, 1, 0))
        lane_i = lax.broadcasted_iota(jnp.int32, (TILE, 128), 1)
        lane = lane_i.astype(jnp.float32)
        xpl = (lane_i // CY).astype(jnp.float32)
        ypl = (lane_i % CY).astype(jnp.float32)
        wy = gauss(ypl - (yrep + sy)) * scale
        xoff = xrep - xpl
        lhs, rhs = [], []
        for k in range(2):
            a = jnp.where(xoff == (x0 + k * BX).astype(jnp.float32) - sx, wy, 0.0)
            lhs.extend(hi_lo(a))
            f = fmat[pl.ds(x0 + k * BX, BX)].reshape(BP, 3 * NZ)
            rhs.extend([f, f])
        g = jnp.dot(jnp.concatenate(lhs, axis=1), jnp.concatenate(rhs, axis=0), preferred_element_type=jnp.float32)
        sums = [None] * 3
        for q in range(NZ // 128):
            wz = gauss(lane + (128.0 * q) - zrep) * scale
            for c in range(3):
                t = g[:, c * NZ + 128 * q : c * NZ + 128 * (q + 1)] * wz
                sums[c] = t if sums[c] is None else sums[c] + t
        return [jnp.sum(v.T, axis=0, keepdims=True) for v in sums]

    def visit(entries, second):
        got = [contribution(*e) for e in entries]
        for (i, n, x0), rows in zip(entries, got):
            for c in range(3):
                if second is None:
                    out_ref[i, c : c + 1, :] += rows[c]
                else:
                    out_ref[i, c : c + 1, :] = rows[c]

    in_pairs(list_ref, part, 2 * BX, visit)


def main_kernel(
    units_ref,
    list_ref,
    tab_ref,
    pick_ref,
    field_ref,
    ground_ref,
    old_ref,
    acc,
    dens_ref,
    out_ref,
    fmat,
    amat_a,
    amat_b,
    zmat_a,
    zmat_b,
    wide_a,
    wide_b,
    band_ref,
    flow,
):
    step = pl.program_id(0)
    steps = CX // XO

    def filtered(b, wide, chans=(0, 1, 2, 3)):
        base = b * XO
        for q in range(NZ // 128):
            cols = slice(q * 128, (q + 1) * 128)
            for c in chans:
                outs = x_filtered(lambda i: acc[base + i, c * CY : (c + 1) * CY, cols], RAW, XO)
                for o in range(XO):
                    hi, lo = hi_lo(outs[o])
                    rows = slice((c * XO + o) * CY, (c * XO + o + 1) * CY)
                    wide[0, rows, cols] = hi
                    wide[1, rows, cols] = lo

    def finish(b, wide, h):
        cols = slice(h * 256, (h + 1) * 256)
        full = jnp.concatenate([wide[0], wide[0], wide[1]], axis=1)
        dens = jnp.dot(full, band_ref[:, cols], preferred_element_type=jnp.float32)
        dens = dens.reshape(4, XO, CY, 256)
        dens_ref[3, :, :, cols] = dens[3]
        for c in range(3):
            d = dens[c] + dens[3] * field_ref[c : c + 1, cols][None]
            dens_ref[c, :, :, cols] = d
            flow[c, pl.ds(12 + b * XO, XO), :, cols] = d + ground_ref[c : c + 1, cols][None]

    @pl.when(step == 0)
    def _():
        def clear(i, _):
            flow[:, i] = jnp.zeros((3, CY, NZ), jnp.float32)
            flow[:, 12 + CX + i] = jnp.zeros((3, CY, NZ), jnp.float32)
            return 0

        lax.fori_loop(0, 16, clear, 0)
        for i in range(BUCKETS * BX, FROWS):
            fmat[i] = jnp.zeros(fmat.shape[1:], jnp.bfloat16)
        for q in range(NZ // 128):
            row = lax.broadcasted_iota(jnp.int32, (128, NZ), 0) + 128 * q
            col = lax.broadcasted_iota(jnp.int32, (128, NZ), 1)
            hi, lo = hi_lo(gauss((row - col).astype(jnp.float32)))
            band_ref[q * 128 : (q + 1) * 128, :] = hi
            band_ref[NZ + q * 128 : NZ + (q + 1) * 128, :] = lo
            band_ref[2 * NZ + q * 128 : 2 * NZ + (q + 1) * 128, :] = hi
        accumulate(units_ref, tab_ref, pick_ref, acc, (amat_a, amat_b), (zmat_a, zmat_b))
        filtered(0, wide_a)

    for parity, now, later in ((1, wide_a, wide_b), (0, wide_b, wide_a)):

        @pl.when((step > 0) & (step <= steps) & (step % 2 == parity))
        def _(now=now, later=later):
            ahead = jnp.minimum(step, steps - 1)
            finish(step - 1, now, 0)
            filtered(ahead, later, (0, 1))
            finish(step - 1, now, 1)
            filtered(ahead, later, (2, 3))

    @pl.when(step > steps)
    def _():
        def block(b, _):
            for c in range(3):

                def chunk(j, _, c=c):
                    cols = pl.ds(pl.multiple_of(j * 128, 128), 128)
                    dest = pl.ds(pl.multiple_of(c * NZ + j * 128, 128), 128)
                    outs = x_filtered(lambda i: flow[c, b * BX + i, :, cols], UNIT, BX)
                    for o in range(BX):
                        fmat[b * BX + o, :, dest] = outs[o].astype(jnp.bfloat16)
                    return 0

                lax.fori_loop(0, NZ // 128, chunk, 0)
            return 0

        lax.fori_loop(0, BUCKETS, block, 0)
        sampled(list_ref, 0, tab_ref, pick_ref, fmat, out_ref)


def sample_own_kernel(part, list_ref, tab_ref, pick_ref, fmat, out_ref):
    sampled(list_ref, part, tab_ref, pick_ref, fmat, out_ref)


def smem():
    return pl.BlockSpec(memory_space=pltpu.SMEM)


def whole(shape):
    return pl.BlockSpec(shape, lambda i: (0,) * len(shape))


PARAMS = pltpu.CompilerParams(vmem_limit_bytes=16 << 20)
MAIN_PARAMS = pltpu.CompilerParams(vmem_limit_bytes=32 << 20)


def factor_scratch():
    return [pltpu.VMEM((4 * BP, 2 * TILE), jnp.bfloat16)] * 2 + [pltpu.VMEM((2 * TILE, NZ), jnp.bfloat16)] * 2


def spread_own_call(listing, table, pick):
    return pl.pallas_call(
        spread_own_kernel,
        grid=(1,),
        in_specs=[smem(), whole(table.shape), whole(pick.shape)],
        out_specs=pl.BlockSpec(memory_space=pltpu.VMEM),
        out_shape=pltpu.VMEM((XROWS, 4 * CY, NZ), jnp.float32),
        scratch_shapes=factor_scratch(),
        compiler_params=PARAMS,
        cost_estimate=pl.CostEstimate(flops=10**10, transcendentals=0, bytes_accessed=3 * 10**7),
        name="spread_own",
    )(listing, table, pick)


def main_call(units, listing, table, pick, field, ground, old):
    steps = CX // XO
    n = table.shape[0]
    fshape = (FROWS, CY, 3 * NZ)
    return pl.pallas_call(
        main_kernel,
        grid=(steps + 2,),
        in_specs=[smem()] * 2
        + [whole(v.shape) for v in (table, pick, field, ground)]
        + [pl.BlockSpec(memory_space=pltpu.VMEM)],
        out_specs=[
            pl.BlockSpec(memory_space=pltpu.VMEM),
            pl.BlockSpec((4, XO, CY, NZ), lambda i: (0, jnp.clip(i - 1, 0, steps - 1), 0, 0)),
            whole((n, 8, TILE)),
            whole(fshape),
        ],
        input_output_aliases={6: 0},
        out_shape=[
            pltpu.VMEM(old.shape, jnp.float32),
            jax.ShapeDtypeStruct((4, CX, CY, NZ), jnp.float32),
            jax.ShapeDtypeStruct((n, 8, TILE), jnp.float32),
            jax.ShapeDtypeStruct(fshape, jnp.bfloat16),
        ],
        scratch_shapes=factor_scratch()
        + [
            pltpu.VMEM((2, 4 * XO * CY, NZ), jnp.bfloat16),
            pltpu.VMEM((2, 4 * XO * CY, NZ), jnp.bfloat16),
            pltpu.VMEM((3 * NZ, NZ), jnp.bfloat16),
            pltpu.VMEM((3, BUCKETS * BX + 12, CY, NZ), jnp.float32),
        ],
        compiler_params=MAIN_PARAMS,
        cost_estimate=pl.CostEstimate(flops=4 * 10**10, transcendentals=0, bytes_accessed=6 * 10**7),
        name="main",
    )(units, listing, table, pick, field, ground, old)


def sample_own_call(part, listing, table, pick, fmat):
    n = table.shape[0]

    def kernel(*refs):
        sample_own_kernel(part, *refs)

    return pl.pallas_call(
        kernel,
        grid=(1,),
        in_specs=[smem(), whole(table.shape), whole(pick.shape), whole(fmat.shape)],
        out_specs=whole((n, 8, TILE)),
        out_shape=jax.ShapeDtypeStruct((n, 8, TILE), jnp.float32),
        compiler_params=PARAMS,
        cost_estimate=pl.CostEstimate(flops=10**10, transcendentals=0, bytes_accessed=3 * 10**7),
        name="sample_own",
    )(listing, table, pick, fmat)


def reached(x, y, exists, sx, sy):
    ax, ay = x + sx, y + sy
    near = (ax >= 0) & (ax < CX + 2 * REACH) & (ay >= -REACH) & (ay < CY + REACH) & exists
    lo = jnp.min(jnp.where(near, ax, 127), axis=-1).reshape(-1)
    hi = jnp.max(jnp.where(near, ax, -1), axis=-1).reshape(-1)
    return lo, hi


def listed(at, lo, hi, per):
    active = lo <= hi
    k = jnp.arange(lo.shape[0] + 2, dtype=jnp.int32)
    i = k[:-2]
    pos = jnp.sum((i[None, :] < i[:, None]) & active[None, :], axis=1, dtype=jnp.int32)
    code = jnp.where(active, (at * 128 + lo) * 128 + hi, 0)
    spot = jnp.where(active, pos + 2, -1)
    grid = jnp.where(spot[None, :] == k[:, None], code[None, :], 0)
    grid = jnp.where(k[:, None] == 1, active[None, :].astype(jnp.int32), grid)
    return jnp.sum(grid, axis=1) + jnp.where(k == 0, per, 0)


def both_lists(lo, hi, per):
    at = jnp.arange(lo.shape[0], dtype=jnp.int32)
    split = listed(
        jnp.concatenate([at, at]),
        jnp.concatenate([lo, lo + BX]),
        jnp.concatenate([jnp.minimum(hi, lo + BX - 1), hi]),
        per,
    )
    return split, listed(at, lo, hi, per)


def ring(value, steps):
    count = lax.axis_size("stream")
    return lax.ppermute(value, "stream", [(i, (i + steps) % count) for i in range(count)])


def line(value, steps):
    count = lax.axis_size("span")
    first, last = max(0, -steps), min(count, count - steps)
    return lax.ppermute(value, "span", [(i, i + steps) for i in range(first, last)])


def on_device(records, cells, counts, background, field):
    cap = records.shape[3]
    total = 9 * cap
    tiles = total // TILE
    bf16, f32 = jnp.bfloat16, jnp.float32
    slots = jnp.arange(cap, dtype=jnp.int32)
    live = slots[None, :] < counts[0][:, None]
    cell = cells[0]
    z = cell % NZ
    x = jnp.where(live, cell // (CY * NZ), 255)
    y = (cell // NZ) % CY
    row = jnp.arange(8)[None, :, None]
    places = jnp.where(row == 4, x[:, None], jnp.where(row == 5, y[:, None], jnp.where(row == 6, z[:, None] // 16, z[:, None] % 16)))
    outgoing = jnp.where(row < 4, jnp.pad(records[0], ((0, 0), (0, 4), (0, 0))), places.astype(bf16))
    outgoing = outgoing.reshape(3, 3, 8, cap)
    dead = jnp.zeros((8,), bf16).at[4].set(255)[:, None]
    outgoing = jnp.stack([ring(outgoing[0], -1), outgoing[1], ring(outgoing[2], 1)])
    me = lax.axis_index("span")
    spans = lax.axis_size("span")
    has_low, has_high = me > 0, me < spans - 1
    from_high = jnp.where(has_high, line(outgoing[:, 0], -1), dead)
    from_low = jnp.where(has_low, line(outgoing[:, 2], 1), dead)
    inbound = jnp.stack([from_high, outgoing[:, 1], from_low], axis=1)
    inbound = inbound.transpose(2, 0, 1, 3).reshape(8, total)

    gi = inbound[4:].astype(jnp.int32)
    gx, gy, gz = gi[0], gi[1], gi[2] * 16 + gi[3]
    klass = (gy >= REACH).astype(jnp.int32) + (gy >= CY - REACH)
    klass = jnp.where(gx > 200, 3, klass)
    kx = jnp.where(klass == 1, CX - 1 - gx, gx)
    key = ((klass * 256 + kx) * CY + gy) * NZ + gz
    order = jnp.arange(total, dtype=jnp.int32)
    key, order, *vals = lax.sort((key, order) + tuple(inbound[c].astype(f32) for c in range(4)), num_keys=1)
    sz = key % NZ
    sy = key // NZ % CY
    sx = key // (CY * NZ) % 256
    sx = jnp.where(key // (CY * NZ * 256) == 1, CX - 1 - sx, sx)
    packed = jnp.stack(vals + [v.astype(f32) for v in (sx, sy, sz // 16, sz % 16)]).astype(bf16)
    packed = packed.reshape(8, tiles, TILE).transpose(1, 0, 2)

    low = line(packed, 1)
    high = line(packed, -1)
    tx, ty = sx.reshape(tiles, TILE), sy.reshape(tiles, TILE)
    own_units, own_list = both_lists(*reached(tx, ty, tx < 200, REACH, 0), 0)
    three, own_units = lax.optimization_barrier((jnp.stack([low, packed, high]), own_units))
    arrays = jnp.stack([ring(three, 1), three, ring(three, -1)])
    places = arrays[:, :, :, 4:6].astype(jnp.int32)
    shift = jnp.arange(-1, 2, dtype=jnp.int32)
    exists = jnp.stack([has_low, jnp.array(True), has_high])
    exists = exists[None, :] & ~((shift[:, None] == 0) & (shift[None, :] == 0))
    lo, hi = reached(
        places[:, :, :, 0],
        places[:, :, :, 1],
        exists[:, :, None, None],
        CX * shift[:, None, None, None] + REACH,
        CY * shift[None, :, None, None],
    )
    rest_units, rest_list = both_lists(lo, hi, tiles)
    table = arrays.reshape(9 * tiles, 8, TILE)

    pick = jnp.asarray(PICK, bf16)
    half = spread_own_call(own_units, packed, pick)
    _, density, partial, fmat = main_call(rest_units, rest_list, table, pick, field, background, half)
    early = sample_own_call(1, own_list, packed, pick, fmat)
    partial = partial[:, :3].reshape(3, 3, tiles, 3, TILE)
    mixed = partial[1] + ring(partial[2], 1) + ring(partial[0], -1)
    mixed, own_list = lax.optimization_barrier((mixed, own_list))
    late = sample_own_call(2, own_list, packed, pick, fmat)
    mine = (early + late)[:, :3]
    own = mixed[1] + mine + line(mixed[2], 1) + line(mixed[0], -1)
    own = own.transpose(1, 0, 2).reshape(3, total)
    _, *vel = lax.sort((order, own[0], own[1], own[2]), num_keys=1)
    velocity = jnp.stack([v.reshape(9, cap) for v in vel], axis=1)[None]
    return density, velocity


def solution(mesh):
    return jax.shard_map(
        on_device,
        mesh=mesh,
        in_specs=(
            P(("stream", "span"), None, None, None),
            P(("stream", "span"), None, None),
            P(("stream", "span"), None),
            P(),
            P(),
        ),
        out_specs=(P(None, "stream", "span", None), P(("stream", "span"), None, None, None)),
        check_vma=False,
    )
```

```python
import jax
import jax.numpy as jnp
import numpy as np
from jax import lax
from jax.experimental import pallas as pl
from jax.experimental.pallas import tpu as pltpu
from jax.sharding import PartitionSpec as P

CX = 64
CY = 16
NZ = 512
REACH = 6
TILE = 128
BX = 8
XO = 8
XROWS = 84
BUCKETS = 10
FROWS = 92
GROUP_D = 4
GROUP_V = 4
BP = BX * CY

spread_width = 12.5


OFFSETS = np.arange(-6, 7).astype(np.float32)
RAW = np.exp(-OFFSETS * OFFSETS / np.float32(spread_width))
SCALE = np.float32(1.0) / np.sum(RAW)
UNIT = RAW * SCALE
PICK = np.zeros((8, 384), np.float32)
PICK[6, :128], PICK[7, :128], PICK[5, 128:256], PICK[4, 256:] = 16.0, 1.0, 1.0, 1.0


def gauss(d):
    return jnp.where(jnp.abs(d) < REACH + 0.5, jnp.exp(d * d * (-1.0 / spread_width)), 0.0)


def hi_lo(v):
    hi = v.astype(jnp.bfloat16)
    lo = (v - hi.astype(jnp.float32)).astype(jnp.bfloat16)
    return hi, lo


def columns(xt, pick):
    return lax.dot_general(
        xt.astype(jnp.bfloat16), pick, (((0,), (0,)), ((), ())), preferred_element_type=jnp.float32
    )


def x_filtered(load, taps, count):
    taps = [float(t) for t in taps]
    outs = []
    ins = [load(i) for i in range(count + 12)]
    for o in range(count):
        total = taps[6] * ins[o + 6]
        for k in range(1, 7):
            total = total + taps[6 + k] * (ins[o + 6 - k] + ins[o + 6 + k])
        outs.append(total)
    return outs


def tile_codes(list_ref, k):
    code = list_ref[k + 2]
    i = code >> 14
    per = list_ref[0]
    n = jnp.where(per == 0, 4, lax.div(i, jnp.maximum(per, 1)))
    return i, n, (code >> 7) & 127, code & 127


def in_groups(list_ref, part, size, width, visit):
    count = list_ref[1]
    middle = (count + 1) // 2
    begin = middle if part == 2 else 0
    end = middle if part == 1 else count

    def group(p, _):
        k = begin + size * p
        visit([tile_codes(list_ref, jnp.minimum(k + j, end - 1))[:3] for j in range(size)], end - k)

        def leftover(t, _):
            i, n, first, last = tile_codes(list_ref, k + t)

            def window(w, _):
                visit([(i, n, first + w * width)], None)
                return 0

            lax.fori_loop(1, (last - first) // width + 1, window, 0)
            return 0

        lax.fori_loop(0, jnp.minimum(end - k, size), leftover, 0)
        return 0

    lax.fori_loop(0, (end - begin + size - 1) // size, group, 0)


def framed(tab_ref, i, n):
    xt = tab_ref[i].astype(jnp.float32)
    row, col = lax.div(n, 3), lax.rem(n, 3)
    sx = ((row - 1) * CX + REACH).astype(jnp.float32)
    sy = ((col - 1) * CY).astype(jnp.float32)
    return xt, sx, sy


def accumulate(list_ref, tab_ref, pick_ref, acc, amats, zmats):
    def factors(i, n, x0, amat, zmat, keep):
        xt, sx, sy = framed(tab_ref, i, n)
        zrep = columns(xt, pick_ref[:, 0:128])
        lane = lax.broadcasted_iota(jnp.int32, (TILE, 128), 1).astype(jnp.float32)
        for q in range(NZ // 128):
            hit = jnp.where(lane + (128.0 * q) == zrep, 1.0, 0.0).astype(jnp.bfloat16)
            cols = slice(128 * q, 128 * (q + 1))
            zmat[0:TILE, cols] = hit
            zmat[TILE : 2 * TILE, cols] = hit
        ypl = lax.broadcasted_iota(jnp.int32, (CY, TILE), 0).astype(jnp.float32)
        gy = gauss(ypl - (xt[5:6, :] + sy))
        if keep is not None:
            gy = jnp.where(keep, gy, 0.0)
        xrow = jnp.broadcast_to(xt[4:5, :] + sx, (CY, TILE))
        parts = [hi_lo(gy * xt[c : c + 1, :]) for c in range(4)]
        for xx in range(BX):
            m = jnp.where(xrow == (x0 + xx).astype(jnp.float32), 1.0, 0.0).astype(jnp.bfloat16)
            for c in range(4):
                rows = slice((xx * 4 + c) * CY, (xx * 4 + c + 1) * CY)
                amat[rows, 0:TILE] = parts[c][0] * m
                amat[rows, TILE : 2 * TILE] = parts[c][1] * m

    def visit(entries, valid):
        for j, (i, n, x0) in enumerate(entries):
            factors(i, n, x0, amats[j], zmats[j], None if j == 0 else j < valid)
        for j, (i, n, x0) in enumerate(entries):
            part = jnp.dot(amats[j][...], zmats[j][...], preferred_element_type=jnp.float32)
            acc[pl.ds(x0, BX)] += part.reshape(BX, 4 * CY, NZ)

    in_groups(list_ref, 0, GROUP_D, BX, visit)


def spread_own_kernel(list_ref, tab_ref, pick_ref, acc, *mats):
    def clear(i, _):
        acc[i] = jnp.zeros(acc.shape[1:], jnp.float32)
        return 0

    lax.fori_loop(0, XROWS, clear, 0)
    accumulate(list_ref, tab_ref, pick_ref, acc, mats[:GROUP_D], mats[GROUP_D:])


def sampled(list_ref, part, tab_ref, pick_ref, fmat, out_ref):
    scale = float(SCALE)
    out_ref[...] = jnp.zeros(out_ref.shape, jnp.float32)

    def contribution(i, n, x0):
        xt, sx, sy = framed(tab_ref, i, n)
        cols = columns(xt, pick_ref[...])
        xrep, yrep, zrep = (cols[:, 128 * k : 128 * (k + 1)] for k in (2, 1, 0))
        lane_i = lax.broadcasted_iota(jnp.int32, (TILE, 128), 1)
        lane = lane_i.astype(jnp.float32)
        xpl = (lane_i // CY).astype(jnp.float32)
        ypl = (lane_i % CY).astype(jnp.float32)
        wy = gauss(ypl - (yrep + sy)) * scale
        xoff = xrep - xpl
        lhs, rhs = [], []
        for k in range(2):
            a = jnp.where(xoff == (x0 + k * BX).astype(jnp.float32) - sx, wy, 0.0)
            lhs.extend(hi_lo(a))
            f = fmat[pl.ds(x0 + k * BX, BX)].reshape(BP, 3 * NZ)
            rhs.extend([f, f])
        g = jnp.dot(jnp.concatenate(lhs, axis=1), jnp.concatenate(rhs, axis=0), preferred_element_type=jnp.float32)
        sums = [None] * 3
        for q in range(NZ // 128):
            wz = gauss(lane + (128.0 * q) - zrep) * scale
            for c in range(3):
                t = g[:, c * NZ + 128 * q : c * NZ + 128 * (q + 1)] * wz
                sums[c] = t if sums[c] is None else sums[c] + t
        return [jnp.sum(v.T, axis=0, keepdims=True) for v in sums]

    def visit(entries, valid):
        got = [contribution(*e) for e in entries]
        for (i, n, x0), rows in zip(entries, got):
            for c in range(3):
                if valid is None:
                    out_ref[i, c : c + 1, :] += rows[c]
                else:
                    out_ref[i, c : c + 1, :] = rows[c]

    in_groups(list_ref, part, GROUP_V, 2 * BX, visit)


def main_kernel(
    units_ref,
    list_ref,
    tab_ref,
    pick_ref,
    field_ref,
    ground_ref,
    old_ref,
    acc,
    dens_ref,
    out_ref,
    fmat,
    wide_a,
    wide_b,
    band_ref,
    flow,
    *mats,
):
    step = pl.program_id(0)
    steps = CX // XO

    def filtered(b, wide, chans=(0, 1, 2, 3)):
        base = b * XO
        for q in range(NZ // 128):
            cols = slice(q * 128, (q + 1) * 128)
            for c in chans:
                outs = x_filtered(lambda i: acc[base + i, c * CY : (c + 1) * CY, cols], RAW, XO)
                for o in range(XO):
                    hi, lo = hi_lo(outs[o])
                    rows = slice((c * XO + o) * CY, (c * XO + o + 1) * CY)
                    wide[0, rows, cols] = hi
                    wide[1, rows, cols] = lo

    def finish(b, wide, h):
        cols = slice(h * 256, (h + 1) * 256)
        full = jnp.concatenate([wide[0], wide[0], wide[1]], axis=1)
        dens = jnp.dot(full, band_ref[:, cols], preferred_element_type=jnp.float32)
        dens = dens.reshape(4, XO, CY, 256)
        dens_ref[3, :, :, cols] = dens[3]
        for c in range(3):
            d = dens[c] + dens[3] * field_ref[c : c + 1, cols][None]
            dens_ref[c, :, :, cols] = d
            flow[c, pl.ds(12 + b * XO, XO), :, cols] = d + ground_ref[c : c + 1, cols][None]

    @pl.when(step == 0)
    def _():
        def clear(i, _):
            flow[:, i] = jnp.zeros((3, CY, NZ), jnp.float32)
            flow[:, 12 + CX + i] = jnp.zeros((3, CY, NZ), jnp.float32)
            return 0

        lax.fori_loop(0, 16, clear, 0)
        for i in range(BUCKETS * BX, FROWS):
            fmat[i] = jnp.zeros(fmat.shape[1:], jnp.bfloat16)
        for q in range(NZ // 128):
            row = lax.broadcasted_iota(jnp.int32, (128, NZ), 0) + 128 * q
            col = lax.broadcasted_iota(jnp.int32, (128, NZ), 1)
            hi, lo = hi_lo(gauss((row - col).astype(jnp.float32)))
            band_ref[q * 128 : (q + 1) * 128, :] = hi
            band_ref[NZ + q * 128 : NZ + (q + 1) * 128, :] = lo
            band_ref[2 * NZ + q * 128 : 2 * NZ + (q + 1) * 128, :] = hi
        accumulate(units_ref, tab_ref, pick_ref, acc, mats[:GROUP_D], mats[GROUP_D:])
        filtered(0, wide_a)

    for parity, now, later in ((1, wide_a, wide_b), (0, wide_b, wide_a)):

        @pl.when((step > 0) & (step <= steps) & (step % 2 == parity))
        def _(now=now, later=later):
            ahead = jnp.minimum(step, steps - 1)
            finish(step - 1, now, 0)
            filtered(ahead, later, (0, 1))
            finish(step - 1, now, 1)
            filtered(ahead, later, (2, 3))

    @pl.when(step > steps)
    def _():
        def block(b, _):
            for c in range(3):
                for j in range(NZ // 128):
                    cols = slice(j * 128, (j + 1) * 128)
                    outs = x_filtered(lambda i: flow[c, b * BX + i, :, cols], UNIT, BX)
                    for o in range(BX):
                        fmat[b * BX + o, :, c * NZ + j * 128 : c * NZ + (j + 1) * 128] = outs[o].astype(jnp.bfloat16)
            return 0

        lax.fori_loop(0, BUCKETS, block, 0)
        sampled(list_ref, 0, tab_ref, pick_ref, fmat, out_ref)


def sample_own_kernel(part, list_ref, tab_ref, pick_ref, fmat, out_ref):
    sampled(list_ref, part, tab_ref, pick_ref, fmat, out_ref)


def smem():
    return pl.BlockSpec(memory_space=pltpu.SMEM)


def whole(shape):
    return pl.BlockSpec(shape, lambda i: (0,) * len(shape))


PARAMS = pltpu.CompilerParams(vmem_limit_bytes=16 << 20)
MAIN_PARAMS = pltpu.CompilerParams(vmem_limit_bytes=32 << 20)


def factor_scratch():
    return [pltpu.VMEM((4 * BP, 2 * TILE), jnp.bfloat16)] * GROUP_D + [
        pltpu.VMEM((2 * TILE, NZ), jnp.bfloat16)
    ] * GROUP_D


def spread_own_call(listing, table, pick):
    return pl.pallas_call(
        spread_own_kernel,
        grid=(1,),
        in_specs=[smem(), whole(table.shape), whole(pick.shape)],
        out_specs=pl.BlockSpec(memory_space=pltpu.VMEM),
        out_shape=pltpu.VMEM((XROWS, 4 * CY, NZ), jnp.float32),
        scratch_shapes=factor_scratch(),
        compiler_params=PARAMS,
        cost_estimate=pl.CostEstimate(flops=10**10, transcendentals=0, bytes_accessed=3 * 10**7),
        name="spread_own",
    )(listing, table, pick)


def main_call(units, listing, table, pick, field, ground, old):
    steps = CX // XO
    n = table.shape[0]
    fshape = (FROWS, CY, 3 * NZ)
    return pl.pallas_call(
        main_kernel,
        grid=(steps + 2,),
        in_specs=[smem()] * 2
        + [whole(v.shape) for v in (table, pick, field, ground)]
        + [pl.BlockSpec(memory_space=pltpu.VMEM)],
        out_specs=[
            pl.BlockSpec(memory_space=pltpu.VMEM),
            pl.BlockSpec((4, XO, CY, NZ), lambda i: (0, jnp.clip(i - 1, 0, steps - 1), 0, 0)),
            whole((n, 8, TILE)),
            whole(fshape),
        ],
        input_output_aliases={6: 0},
        out_shape=[
            pltpu.VMEM(old.shape, jnp.float32),
            jax.ShapeDtypeStruct((4, CX, CY, NZ), jnp.float32),
            jax.ShapeDtypeStruct((n, 8, TILE), jnp.float32),
            jax.ShapeDtypeStruct(fshape, jnp.bfloat16),
        ],
        scratch_shapes=[
            pltpu.VMEM((2, 4 * XO * CY, NZ), jnp.bfloat16),
            pltpu.VMEM((2, 4 * XO * CY, NZ), jnp.bfloat16),
            pltpu.VMEM((3 * NZ, NZ), jnp.bfloat16),
            pltpu.VMEM((3, BUCKETS * BX + 12, CY, NZ), jnp.float32),
        ]
        + factor_scratch(),
        compiler_params=MAIN_PARAMS,
        cost_estimate=pl.CostEstimate(flops=4 * 10**10, transcendentals=0, bytes_accessed=6 * 10**7),
        name="main",
    )(units, listing, table, pick, field, ground, old)


def sample_own_call(part, listing, table, pick, fmat):
    n = table.shape[0]

    def kernel(*refs):
        sample_own_kernel(part, *refs)

    return pl.pallas_call(
        kernel,
        grid=(1,),
        in_specs=[smem(), whole(table.shape), whole(pick.shape), whole(fmat.shape)],
        out_specs=whole((n, 8, TILE)),
        out_shape=jax.ShapeDtypeStruct((n, 8, TILE), jnp.float32),
        compiler_params=PARAMS,
        cost_estimate=pl.CostEstimate(flops=10**10, transcendentals=0, bytes_accessed=3 * 10**7),
        name="sample_own",
    )(listing, table, pick, fmat)


def reached(x, y, exists, sx, sy):
    ax, ay = x + sx, y + sy
    near = (ax >= 0) & (ax < CX + 2 * REACH) & (ay >= -REACH) & (ay < CY + REACH) & exists
    lo = jnp.min(jnp.where(near, ax, 127), axis=-1).reshape(-1)
    hi = jnp.max(jnp.where(near, ax, -1), axis=-1).reshape(-1)
    return lo, hi


def listed(at, lo, hi, per):
    active = lo <= hi
    k = jnp.arange(lo.shape[0] + 2, dtype=jnp.int32)
    i = k[:-2]
    pos = jnp.sum((i[None, :] < i[:, None]) & active[None, :], axis=1, dtype=jnp.int32)
    code = jnp.where(active, (at * 128 + lo) * 128 + hi, 0)
    spot = jnp.where(active, pos + 2, -1)
    grid = jnp.where(spot[None, :] == k[:, None], code[None, :], 0)
    grid = jnp.where(k[:, None] == 1, active[None, :].astype(jnp.int32), grid)
    return jnp.sum(grid, axis=1) + jnp.where(k == 0, per, 0)


def both_lists(lo, hi, per):
    at = jnp.arange(lo.shape[0], dtype=jnp.int32)
    split = listed(
        jnp.concatenate([at, at]),
        jnp.concatenate([lo, lo + BX]),
        jnp.concatenate([jnp.minimum(hi, lo + BX - 1), hi]),
        per,
    )
    return split, listed(at, lo, hi, per)


def ring(value, steps):
    count = lax.axis_size("stream")
    return lax.ppermute(value, "stream", [(i, (i + steps) % count) for i in range(count)])


def line(value, steps):
    count = lax.axis_size("span")
    first, last = max(0, -steps), min(count, count - steps)
    return lax.ppermute(value, "span", [(i, i + steps) for i in range(first, last)])


def on_device(records, cells, counts, background, field):
    cap = records.shape[3]
    total = 9 * cap
    tiles = total // TILE
    bf16, f32 = jnp.bfloat16, jnp.float32
    slots = jnp.arange(cap, dtype=jnp.int32)
    live = slots[None, :] < counts[0][:, None]
    cell = cells[0]
    z = cell % NZ
    x = jnp.where(live, cell // (CY * NZ), 255)
    y = (cell // NZ) % CY
    row = jnp.arange(8)[None, :, None]
    places = jnp.where(row == 4, x[:, None], jnp.where(row == 5, y[:, None], jnp.where(row == 6, z[:, None] // 16, z[:, None] % 16)))
    outgoing = jnp.where(row < 4, jnp.pad(records[0], ((0, 0), (0, 4), (0, 0))), places.astype(bf16))
    outgoing = outgoing.reshape(3, 3, 8, cap)
    dead = jnp.zeros((8,), bf16).at[4].set(255)[:, None]
    outgoing = jnp.stack([ring(outgoing[0], -1), outgoing[1], ring(outgoing[2], 1)])
    me = lax.axis_index("span")
    spans = lax.axis_size("span")
    has_low, has_high = me > 0, me < spans - 1
    from_high = jnp.where(has_high, line(outgoing[:, 0], -1), dead)
    from_low = jnp.where(has_low, line(outgoing[:, 2], 1), dead)
    inbound = jnp.stack([from_high, outgoing[:, 1], from_low], axis=1)
    inbound = inbound.transpose(2, 0, 1, 3).reshape(8, total)

    gi = inbound[4:].astype(jnp.int32)
    gx, gy, gz = gi[0], gi[1], gi[2] * 16 + gi[3]
    klass = (gy >= REACH).astype(jnp.int32) + (gy >= CY - REACH)
    klass = jnp.where(gx > 200, 3, klass)
    kx = jnp.where(klass == 1, CX - 1 - gx, gx)
    key = ((klass * 256 + kx) * CY + gy) * NZ + gz
    order = jnp.arange(total, dtype=jnp.int32)
    key, order, *vals = lax.sort((key, order) + tuple(inbound[c].astype(f32) for c in range(4)), num_keys=1)
    sz = key % NZ
    sy = key // NZ % CY
    sx = key // (CY * NZ) % 256
    sx = jnp.where(key // (CY * NZ * 256) == 1, CX - 1 - sx, sx)
    packed = jnp.stack(vals + [v.astype(f32) for v in (sx, sy, sz // 16, sz % 16)]).astype(bf16)
    packed = packed.reshape(8, tiles, TILE).transpose(1, 0, 2)

    low = line(packed, 1)
    high = line(packed, -1)
    tx, ty = sx.reshape(tiles, TILE), sy.reshape(tiles, TILE)
    own_units, own_list = both_lists(*reached(tx, ty, tx < 200, REACH, 0), 0)
    three, own_units = lax.optimization_barrier((jnp.stack([low, packed, high]), own_units))
    arrays = jnp.stack([ring(three, 1), three, ring(three, -1)])
    places = arrays[:, :, :, 4:6].astype(jnp.int32)
    shift = jnp.arange(-1, 2, dtype=jnp.int32)
    exists = jnp.stack([has_low, jnp.array(True), has_high])
    exists = exists[None, :] & ~((shift[:, None] == 0) & (shift[None, :] == 0))
    lo, hi = reached(
        places[:, :, :, 0],
        places[:, :, :, 1],
        exists[:, :, None, None],
        CX * shift[:, None, None, None] + REACH,
        CY * shift[None, :, None, None],
    )
    rest_units, rest_list = both_lists(lo, hi, tiles)
    table = arrays.reshape(9 * tiles, 8, TILE)

    pick = jnp.asarray(PICK, bf16)
    half = spread_own_call(own_units, packed, pick)
    _, density, partial, fmat = main_call(rest_units, rest_list, table, pick, field, background, half)
    early = sample_own_call(1, own_list, packed, pick, fmat)
    partial = partial[:, :3].reshape(3, 3, tiles, 3, TILE)
    mixed = partial[1] + ring(partial[2], 1) + ring(partial[0], -1)
    mixed, own_list = lax.optimization_barrier((mixed, own_list))
    late = sample_own_call(2, own_list, packed, pick, fmat)
    mine = (early + late)[:, :3]
    own = mixed[1] + mine + line(mixed[2], 1) + line(mixed[0], -1)
    own = own.transpose(1, 0, 2).reshape(3, total)
    _, *vel = lax.sort((order, own[0], own[1], own[2]), num_keys=1)
    velocity = jnp.stack([v.reshape(9, cap) for v in vel], axis=1)[None]
    return density, velocity


def solution(mesh):
    return jax.shard_map(
        on_device,
        mesh=mesh,
        in_specs=(
            P(("stream", "span"), None, None, None),
            P(("stream", "span"), None, None),
            P(("stream", "span"), None),
            P(),
            P(),
        ),
        out_specs=(P(None, "stream", "span", None), P(("stream", "span"), None, None, None)),
        check_vma=False,
    )
```

```python
import jax
import jax.numpy as jnp
import numpy as np
from jax import lax
from jax.experimental import pallas as pl
from jax.experimental.pallas import tpu as pltpu
from jax.sharding import PartitionSpec as P

CX = 64
CY = 16
NZ = 512
REACH = 6
TILE = 128
BX = 8
XO = 8
XROWS = 84
BUCKETS = 10
FROWS = 92
ZW = 384
GROUP_D = 6
GROUP_V = 4
BP = BX * CY

spread_width = 12.5


OFFSETS = np.arange(-6, 7).astype(np.float32)
RAW = np.exp(-OFFSETS * OFFSETS / np.float32(spread_width))
SCALE = np.float32(1.0) / np.sum(RAW)
UNIT = RAW * SCALE
PICK = np.zeros((8, 384), np.float32)
PICK[6, :128], PICK[7, :128], PICK[5, 128:256], PICK[4, 256:] = 16.0, 1.0, 1.0, 1.0


def gauss(d):
    return jnp.where(jnp.abs(d) < REACH + 0.5, jnp.exp(d * d * (-1.0 / spread_width)), 0.0)


def hi_lo(v):
    hi = v.astype(jnp.bfloat16)
    lo = (v - hi.astype(jnp.float32)).astype(jnp.bfloat16)
    return hi, lo


def columns(xt, pick):
    return lax.dot_general(
        xt.astype(jnp.bfloat16), pick, (((0,), (0,)), ((), ())), preferred_element_type=jnp.float32
    )


def x_filtered(load, taps, count):
    taps = [float(t) for t in taps]
    outs = []
    ins = [load(i) for i in range(count + 12)]
    for o in range(count):
        total = taps[6] * ins[o + 6]
        for k in range(1, 7):
            total = total + taps[6 + k] * (ins[o + 6 - k] + ins[o + 6 + k])
        outs.append(total)
    return outs


def tile_codes(list_ref, k):
    code = list_ref[k + 2]
    i = code >> 14
    per = list_ref[0]
    n = jnp.where(per == 0, 4, lax.div(i, jnp.maximum(per, 1)))
    return i, n, (code >> 7) & 127, code & 127


def in_groups(list_ref, part, size, width, visit):
    count = list_ref[1]
    middle = (count + 1) // 2
    begin = middle if part == 2 else 0
    end = middle if part == 1 else count

    def group(p, _):
        k = begin + size * p
        visit([tile_codes(list_ref, jnp.minimum(k + j, end - 1))[:3] for j in range(size)], end - k)

        def leftover(t, _):
            i, n, first, last = tile_codes(list_ref, k + t)

            def window(w, _):
                visit([(i, n, first + w * width)], None)
                return 0

            lax.fori_loop(1, (last - first) // width + 1, window, 0)
            return 0

        lax.fori_loop(0, jnp.minimum(end - k, size), leftover, 0)
        return 0

    lax.fori_loop(0, (end - begin + size - 1) // size, group, 0)


def framed(tab_ref, i, n):
    xt = tab_ref[i].astype(jnp.float32)
    row, col = lax.div(n, 3), lax.rem(n, 3)
    sx = ((row - 1) * CX + REACH).astype(jnp.float32)
    sy = ((col - 1) * CY).astype(jnp.float32)
    return xt, sx, sy


def accumulate(list_ref, tab_ref, pick_ref, acc, amats, zmats):
    def factors(i, n, x0, amat, zmat, keep):
        xt, sx, sy = framed(tab_ref, i, n)
        zrep = columns(xt, pick_ref[:, 0:128])
        lane = lax.broadcasted_iota(jnp.int32, (TILE, 128), 1).astype(jnp.float32)
        for q in range(NZ // 128):
            hit = jnp.where(lane + (128.0 * q) == zrep, 1.0, 0.0).astype(jnp.bfloat16)
            cols = slice(128 * q, 128 * (q + 1))
            zmat[0:TILE, cols] = hit
            zmat[TILE : 2 * TILE, cols] = hit
        ypl = lax.broadcasted_iota(jnp.int32, (CY, TILE), 0).astype(jnp.float32)
        gy = gauss(ypl - (xt[5:6, :] + sy))
        if keep is not None:
            gy = jnp.where(keep, gy, 0.0)
        xrow = jnp.broadcast_to(xt[4:5, :] + sx, (CY, TILE))
        parts = [hi_lo(gy * xt[c : c + 1, :]) for c in range(4)]
        for xx in range(BX):
            m = jnp.where(xrow == (x0 + xx).astype(jnp.float32), 1.0, 0.0).astype(jnp.bfloat16)
            for c in range(4):
                rows = slice((xx * 4 + c) * CY, (xx * 4 + c + 1) * CY)
                amat[rows, 0:TILE] = parts[c][0] * m
                amat[rows, TILE : 2 * TILE] = parts[c][1] * m

    def visit(entries, valid):
        for j, (i, n, x0) in enumerate(entries):
            factors(i, n, x0, amats[j], zmats[j], None if j == 0 else j < valid)
        for j, (i, n, x0) in enumerate(entries):
            part = jnp.dot(amats[j][...], zmats[j][...], preferred_element_type=jnp.float32)
            acc[pl.ds(x0, BX)] += part.reshape(BX, 4 * CY, NZ)

    in_groups(list_ref, 0, GROUP_D, BX, visit)


def spread_own_kernel(list_ref, tab_ref, pick_ref, out_ref, acc, sem, *mats):
    def clear(i, _):
        acc[i] = jnp.zeros(acc.shape[1:], jnp.float32)
        return 0

    lax.fori_loop(0, XROWS, clear, 0)
    accumulate(list_ref, tab_ref, pick_ref, acc, mats[:GROUP_D], mats[GROUP_D:])
    copy = pltpu.make_async_copy(acc, out_ref, sem)
    copy.start()
    copy.wait()


def sampled(list_ref, part, tab_ref, pick_ref, fmat, out_ref):
    scale = float(SCALE)
    out_ref[...] = jnp.zeros(out_ref.shape, jnp.float32)

    def contribution(i, n, x0):
        xt, sx, sy = framed(tab_ref, i, n)
        cols = columns(xt, pick_ref[...])
        xrep, yrep, zrep = (cols[:, 128 * k : 128 * (k + 1)] for k in (2, 1, 0))
        lane_i = lax.broadcasted_iota(jnp.int32, (TILE, 128), 1)
        lane = lane_i.astype(jnp.float32)
        xpl = (lane_i // CY).astype(jnp.float32)
        ypl = (lane_i % CY).astype(jnp.float32)
        wy = gauss(ypl - (yrep + sy)) * scale
        xoff = xrep - xpl
        lhs, rhs = [], []
        for k in range(2):
            a = jnp.where(xoff == (x0 + k * BX).astype(jnp.float32) - sx, wy, 0.0)
            lhs.extend(hi_lo(a))
            f = fmat[pl.ds(x0 + k * BX, BX)].reshape(BP, 3 * NZ)
            rhs.extend([f, f])
        g = jnp.dot(jnp.concatenate(lhs, axis=1), jnp.concatenate(rhs, axis=0), preferred_element_type=jnp.float32)
        sums = [None] * 3
        for q in range(NZ // 128):
            wz = gauss(lane + (128.0 * q) - zrep) * scale
            for c in range(3):
                t = g[:, c * NZ + 128 * q : c * NZ + 128 * (q + 1)] * wz
                sums[c] = t if sums[c] is None else sums[c] + t
        return [jnp.sum(v.T, axis=0, keepdims=True) for v in sums]

    def visit(entries, valid):
        got = [contribution(*e) for e in entries]
        for (i, n, x0), rows in zip(entries, got):
            for c in range(3):
                if valid is None:
                    out_ref[i, c : c + 1, :] += rows[c]
                else:
                    out_ref[i, c : c + 1, :] = rows[c]

    in_groups(list_ref, part, GROUP_V, 2 * BX, visit)


def main_kernel(
    units_ref,
    list_ref,
    tab_ref,
    pick_ref,
    field_ref,
    ground_ref,
    old_ref,
    dens_ref,
    out_ref,
    fmat,
    acc,
    sem,
    wide_a,
    wide_b,
    band_ref,
    flow,
    *mats,
):
    step = pl.program_id(0)
    steps = CX // XO

    def filtered(b, wide, chans=(0, 1, 2, 3)):
        base = b * XO
        for q in range(NZ // 128):
            cols = slice(q * 128, (q + 1) * 128)
            for c in chans:
                outs = x_filtered(lambda i: acc[base + i, c * CY : (c + 1) * CY, cols], RAW, XO)
                for o in range(XO):
                    hi, lo = hi_lo(outs[o])
                    rows = slice((c * XO + o) * CY, (c * XO + o + 1) * CY)
                    wide[0, rows, cols] = hi
                    wide[1, rows, cols] = lo

    def finish(b, wide, h):
        cols = slice(h * 256, (h + 1) * 256)
        zs = slice(h * 128, h * 128 + ZW)
        full = jnp.concatenate([wide[0, :, zs], wide[0, :, zs], wide[1, :, zs]], axis=1)
        dens = jnp.dot(full, band_ref[h], preferred_element_type=jnp.float32)
        dens = dens.reshape(4, XO, CY, 256)
        dens_ref[3, :, :, cols] = dens[3]
        for c in range(3):
            d = dens[c] + dens[3] * field_ref[c : c + 1, cols][None]
            dens_ref[c, :, :, cols] = d
            flow[c, pl.ds(12 + b * XO, XO), :, cols] = d + ground_ref[c : c + 1, cols][None]

    @pl.when(step == 0)
    def _():
        copy = pltpu.make_async_copy(old_ref, acc, sem)
        copy.start()

        def clear(i, _):
            flow[:, i] = jnp.zeros((3, CY, NZ), jnp.float32)
            flow[:, 12 + CX + i] = jnp.zeros((3, CY, NZ), jnp.float32)
            return 0

        lax.fori_loop(0, 16, clear, 0)
        for i in range(BUCKETS * BX, FROWS):
            fmat[i] = jnp.zeros(fmat.shape[1:], jnp.bfloat16)
        for h in range(2):
            for q in range(3):
                row = lax.broadcasted_iota(jnp.int32, (128, 256), 0) + 128 * (q + h)
                col = lax.broadcasted_iota(jnp.int32, (128, 256), 1) + 256 * h
                hi, lo = hi_lo(gauss((row - col).astype(jnp.float32)))
                band_ref[h, q * 128 : (q + 1) * 128, :] = hi
                band_ref[h, ZW + q * 128 : ZW + (q + 1) * 128, :] = lo
                band_ref[h, 2 * ZW + q * 128 : 2 * ZW + (q + 1) * 128, :] = hi
        copy.wait()
        accumulate(units_ref, tab_ref, pick_ref, acc, mats[:GROUP_D], mats[GROUP_D:])
        filtered(0, wide_a)

    for parity, now, later in ((1, wide_a, wide_b), (0, wide_b, wide_a)):

        @pl.when((step > 0) & (step <= steps) & (step % 2 == parity))
        def _(now=now, later=later):
            ahead = jnp.minimum(step, steps - 1)
            finish(step - 1, now, 0)
            filtered(ahead, later, (0, 1))
            finish(step - 1, now, 1)
            filtered(ahead, later, (2, 3))

    @pl.when(step > steps)
    def _():
        def block(b, _):
            for c in range(3):
                for j in range(NZ // 128):
                    cols = slice(j * 128, (j + 1) * 128)
                    outs = x_filtered(lambda i: flow[c, b * BX + i, :, cols], UNIT, BX)
                    for o in range(BX):
                        fmat[b * BX + o, :, c * NZ + j * 128 : c * NZ + (j + 1) * 128] = outs[o].astype(jnp.bfloat16)
            return 0

        lax.fori_loop(0, BUCKETS, block, 0)
        sampled(list_ref, 0, tab_ref, pick_ref, fmat, out_ref)


def sample_own_kernel(part, list_ref, tab_ref, pick_ref, fmat, out_ref):
    sampled(list_ref, part, tab_ref, pick_ref, fmat, out_ref)


def smem():
    return pl.BlockSpec(memory_space=pltpu.SMEM)


def whole(shape):
    return pl.BlockSpec(shape, lambda i: (0,) * len(shape))


PARAMS = pltpu.CompilerParams(vmem_limit_bytes=24 << 20)
MAIN_PARAMS = pltpu.CompilerParams(vmem_limit_bytes=40 << 20)


def factor_scratch():
    return [pltpu.VMEM((4 * BP, 2 * TILE), jnp.bfloat16)] * GROUP_D + [
        pltpu.VMEM((2 * TILE, NZ), jnp.bfloat16)
    ] * GROUP_D


def spread_own_call(listing, table, pick):
    return pl.pallas_call(
        spread_own_kernel,
        grid=(1,),
        in_specs=[smem(), whole(table.shape), whole(pick.shape)],
        out_specs=pl.BlockSpec(memory_space=pltpu.HBM),
        out_shape=pltpu.HBM((XROWS, 4 * CY, NZ), jnp.float32),
        scratch_shapes=[pltpu.VMEM((XROWS, 4 * CY, NZ), jnp.float32), pltpu.SemaphoreType.DMA] + factor_scratch(),
        compiler_params=PARAMS,
        cost_estimate=pl.CostEstimate(flops=10**10, transcendentals=0, bytes_accessed=3 * 10**7),
        name="spread_own",
    )(listing, table, pick)


def main_call(units, listing, table, pick, field, ground, old):
    steps = CX // XO
    n = table.shape[0]
    fshape = (FROWS, CY, 3 * NZ)
    return pl.pallas_call(
        main_kernel,
        grid=(steps + 2,),
        in_specs=[smem()] * 2
        + [whole(v.shape) for v in (table, pick, field, ground)]
        + [pl.BlockSpec(memory_space=pltpu.HBM)],
        out_specs=[
            pl.BlockSpec((4, XO, CY, NZ), lambda i: (0, jnp.clip(i - 1, 0, steps - 1), 0, 0)),
            whole((n, 8, TILE)),
            whole(fshape),
        ],
        out_shape=[
            jax.ShapeDtypeStruct((4, CX, CY, NZ), jnp.float32),
            jax.ShapeDtypeStruct((n, 8, TILE), jnp.float32),
            jax.ShapeDtypeStruct(fshape, jnp.bfloat16),
        ],
        scratch_shapes=[
            pltpu.VMEM(old.shape, jnp.float32),
            pltpu.SemaphoreType.DMA,
            pltpu.VMEM((2, 4 * XO * CY, NZ), jnp.bfloat16),
            pltpu.VMEM((2, 4 * XO * CY, NZ), jnp.bfloat16),
            pltpu.VMEM((2, 3 * ZW, 256), jnp.bfloat16),
            pltpu.VMEM((3, BUCKETS * BX + 12, CY, NZ), jnp.float32),
        ]
        + factor_scratch(),
        compiler_params=MAIN_PARAMS,
        cost_estimate=pl.CostEstimate(flops=4 * 10**10, transcendentals=0, bytes_accessed=6 * 10**7),
        name="main",
    )(units, listing, table, pick, field, ground, old)


def sample_own_call(part, listing, table, pick, fmat):
    n = table.shape[0]

    def kernel(*refs):
        sample_own_kernel(part, *refs)

    return pl.pallas_call(
        kernel,
        grid=(1,),
        in_specs=[smem(), whole(table.shape), whole(pick.shape), whole(fmat.shape)],
        out_specs=whole((n, 8, TILE)),
        out_shape=jax.ShapeDtypeStruct((n, 8, TILE), jnp.float32),
        compiler_params=PARAMS,
        cost_estimate=pl.CostEstimate(flops=10**10, transcendentals=0, bytes_accessed=3 * 10**7),
        name="sample_own",
    )(listing, table, pick, fmat)


def reached(x, y, exists, sx, sy):
    ax, ay = x + sx, y + sy
    near = (ax >= 0) & (ax < CX + 2 * REACH) & (ay >= -REACH) & (ay < CY + REACH) & exists
    lo = jnp.min(jnp.where(near, ax, 127), axis=-1).reshape(-1)
    hi = jnp.max(jnp.where(near, ax, -1), axis=-1).reshape(-1)
    return lo, hi


def listed(at, lo, hi, per):
    active = lo <= hi
    k = jnp.arange(lo.shape[0] + 2, dtype=jnp.int32)
    i = k[:-2]
    pos = jnp.sum((i[None, :] < i[:, None]) & active[None, :], axis=1, dtype=jnp.int32)
    code = jnp.where(active, (at * 128 + lo) * 128 + hi, 0)
    spot = jnp.where(active, pos + 2, -1)
    grid = jnp.where(spot[None, :] == k[:, None], code[None, :], 0)
    grid = jnp.where(k[:, None] == 1, active[None, :].astype(jnp.int32), grid)
    return jnp.sum(grid, axis=1) + jnp.where(k == 0, per, 0)


def both_lists(lo, hi, per):
    at = jnp.arange(lo.shape[0], dtype=jnp.int32)
    split = listed(
        jnp.concatenate([at, at]),
        jnp.concatenate([lo, lo + BX]),
        jnp.concatenate([jnp.minimum(hi, lo + BX - 1), hi]),
        per,
    )
    return split, listed(at, lo, hi, per)


def ring(value, steps):
    count = lax.axis_size("stream")
    return lax.ppermute(value, "stream", [(i, (i + steps) % count) for i in range(count)])


def line(value, steps):
    count = lax.axis_size("span")
    first, last = max(0, -steps), min(count, count - steps)
    return lax.ppermute(value, "span", [(i, i + steps) for i in range(first, last)])


def on_device(records, cells, counts, background, field):
    cap = records.shape[3]
    total = 9 * cap
    tiles = total // TILE
    bf16, f32 = jnp.bfloat16, jnp.float32
    slots = jnp.arange(cap, dtype=jnp.int32)
    live = slots[None, :] < counts[0][:, None]
    cell = cells[0]
    z = cell % NZ
    x = jnp.where(live, cell // (CY * NZ), 255)
    y = (cell // NZ) % CY
    row = jnp.arange(8)[None, :, None]
    places = jnp.where(row == 4, x[:, None], jnp.where(row == 5, y[:, None], jnp.where(row == 6, z[:, None] // 16, z[:, None] % 16)))
    outgoing = jnp.where(row < 4, jnp.pad(records[0], ((0, 0), (0, 4), (0, 0))), places.astype(bf16))
    outgoing = outgoing.reshape(3, 3, 8, cap)
    dead = jnp.zeros((8,), bf16).at[4].set(255)[:, None]
    outgoing = jnp.stack([ring(outgoing[0], -1), outgoing[1], ring(outgoing[2], 1)])
    me = lax.axis_index("span")
    spans = lax.axis_size("span")
    has_low, has_high = me > 0, me < spans - 1
    from_high = jnp.where(has_high, line(outgoing[:, 0], -1), dead)
    from_low = jnp.where(has_low, line(outgoing[:, 2], 1), dead)
    inbound = jnp.stack([from_high, outgoing[:, 1], from_low], axis=1)
    inbound = inbound.transpose(2, 0, 1, 3).reshape(8, total)

    gi = inbound[4:].astype(jnp.int32)
    gx, gy, gz = gi[0], gi[1], gi[2] * 16 + gi[3]
    klass = (gy >= REACH).astype(jnp.int32) + (gy >= CY - REACH)
    klass = jnp.where(gx > 200, 3, klass)
    kx = jnp.where(klass == 1, CX - 1 - gx, gx)
    key = ((klass * 256 + kx) * CY + gy) * NZ + gz
    order = jnp.arange(total, dtype=jnp.int32)
    key, order, *vals = lax.sort((key, order) + tuple(inbound[c].astype(f32) for c in range(4)), num_keys=1)
    sz = key % NZ
    sy = key // NZ % CY
    sx = key // (CY * NZ) % 256
    sx = jnp.where(key // (CY * NZ * 256) == 1, CX - 1 - sx, sx)
    packed = jnp.stack(vals + [v.astype(f32) for v in (sx, sy, sz // 16, sz % 16)]).astype(bf16)
    packed = packed.reshape(8, tiles, TILE).transpose(1, 0, 2)

    low = line(packed, 1)
    high = line(packed, -1)
    tx, ty = sx.reshape(tiles, TILE), sy.reshape(tiles, TILE)
    own_units, own_list = both_lists(*reached(tx, ty, tx < 200, REACH, 0), 0)
    three, own_units = lax.optimization_barrier((jnp.stack([low, packed, high]), own_units))
    arrays = jnp.stack([ring(three, 1), three, ring(three, -1)])
    places = arrays[:, :, :, 4:6].astype(jnp.int32)
    shift = jnp.arange(-1, 2, dtype=jnp.int32)
    exists = jnp.stack([has_low, jnp.array(True), has_high])
    exists = exists[None, :] & ~((shift[:, None] == 0) & (shift[None, :] == 0))
    lo, hi = reached(
        places[:, :, :, 0],
        places[:, :, :, 1],
        exists[:, :, None, None],
        CX * shift[:, None, None, None] + REACH,
        CY * shift[None, :, None, None],
    )
    rest_units, rest_list = both_lists(lo, hi, tiles)
    table = arrays.reshape(9 * tiles, 8, TILE)

    pick = jnp.asarray(PICK, bf16)
    half = spread_own_call(own_units, packed, pick)
    density, partial, fmat = main_call(rest_units, rest_list, table, pick, field, background, half)
    early = sample_own_call(1, own_list, packed, pick, fmat)
    partial = partial[:, :3].reshape(3, 3, tiles, 3, TILE)
    mixed = partial[1] + ring(partial[2], 1) + ring(partial[0], -1)
    mixed, own_list = lax.optimization_barrier((mixed, own_list))
    late = sample_own_call(2, own_list, packed, pick, fmat)
    mine = (early + late)[:, :3]
    own = mixed[1] + mine + line(mixed[2], 1) + line(mixed[0], -1)
    own = own.transpose(1, 0, 2).reshape(3, total)
    _, *vel = lax.sort((order, own[0], own[1], own[2]), num_keys=1)
    velocity = jnp.stack([v.reshape(9, cap) for v in vel], axis=1)[None]
    return density, velocity


def solution(mesh):
    return jax.shard_map(
        on_device,
        mesh=mesh,
        in_specs=(
            P(("stream", "span"), None, None, None),
            P(("stream", "span"), None, None),
            P(("stream", "span"), None),
            P(),
            P(),
        ),
        out_specs=(P(None, "stream", "span", None), P(("stream", "span"), None, None, None)),
        check_vma=False,
    )
```

```python
import jax
import jax.numpy as jnp
import numpy as np
from jax import lax
from jax.experimental import pallas as pl
from jax.experimental.pallas import tpu as pltpu
from jax.sharding import PartitionSpec as P

CX = 64
CY = 16
NZ = 512
REACH = 6
TILE = 128
BX = 8
XO = 8
XROWS = 84
BUCKETS = 10
FROWS = 92
ZW = 384
GROUP_D = 6
GROUP_V = 4
BP = BX * CY

spread_width = 12.5


OFFSETS = np.arange(-6, 7).astype(np.float32)
RAW = np.exp(-OFFSETS * OFFSETS / np.float32(spread_width))
SCALE = np.float32(1.0) / np.sum(RAW)
UNIT = RAW * SCALE
PICK = np.zeros((8, 384), np.float32)
PICK[6, :128], PICK[7, :128], PICK[5, 128:256], PICK[4, 256:] = 16.0, 1.0, 1.0, 1.0


def gauss(d):
    return jnp.where(jnp.abs(d) < REACH + 0.5, jnp.exp(d * d * (-1.0 / spread_width)), 0.0)


def hi_lo(v):
    hi = v.astype(jnp.bfloat16)
    lo = (v - hi.astype(jnp.float32)).astype(jnp.bfloat16)
    return hi, lo


def columns(xt, pick):
    return lax.dot_general(
        xt.astype(jnp.bfloat16), pick, (((0,), (0,)), ((), ())), preferred_element_type=jnp.float32
    )


def x_filtered(load, taps, count):
    taps = [float(t) for t in taps]
    outs = []
    ins = [load(i) for i in range(count + 12)]
    for o in range(count):
        total = taps[6] * ins[o + 6]
        for k in range(1, 7):
            total = total + taps[6 + k] * (ins[o + 6 - k] + ins[o + 6 + k])
        outs.append(total)
    return outs


def tile_codes(list_ref, k):
    code = list_ref[k + 2]
    i = code >> 14
    per = list_ref[0]
    n = jnp.where(per == 0, 4, lax.div(i, jnp.maximum(per, 1)))
    return i, n, (code >> 7) & 127, code & 127


def in_groups(list_ref, part, size, width, visit):
    count = list_ref[1]
    middle = (count + 1) // 2
    begin = middle if part == 2 else 0
    end = middle if part == 1 else count

    def group(p, _):
        k = begin + size * p
        visit([tile_codes(list_ref, jnp.minimum(k + j, end - 1))[:3] for j in range(size)], end - k)

        def leftover(t, _):
            i, n, first, last = tile_codes(list_ref, k + t)

            def window(w, _):
                visit([(i, n, first + w * width)], None)
                return 0

            lax.fori_loop(1, (last - first) // width + 1, window, 0)
            return 0

        lax.fori_loop(0, jnp.minimum(end - k, size), leftover, 0)
        return 0

    lax.fori_loop(0, (end - begin + size - 1) // size, group, 0)


def framed(tab_ref, i, n):
    xt = tab_ref[i].astype(jnp.float32)
    row, col = lax.div(n, 3), lax.rem(n, 3)
    sx = ((row - 1) * CX + REACH).astype(jnp.float32)
    sy = ((col - 1) * CY).astype(jnp.float32)
    return xt, sx, sy


def accumulate(list_ref, tab_ref, pick_ref, acc, amats, zmats):
    def factors(i, n, x0, amat, zmat, keep):
        xt, sx, sy = framed(tab_ref, i, n)
        zrep = columns(xt, pick_ref[:, 0:128])
        lane = lax.broadcasted_iota(jnp.int32, (TILE, 128), 1).astype(jnp.float32)
        for q in range(NZ // 128):
            hit = jnp.where(lane + (128.0 * q) == zrep, 1.0, 0.0).astype(jnp.bfloat16)
            cols = slice(128 * q, 128 * (q + 1))
            zmat[0:TILE, cols] = hit
            zmat[TILE : 2 * TILE, cols] = hit
        ypl = lax.broadcasted_iota(jnp.int32, (CY, TILE), 0).astype(jnp.float32)
        gy = gauss(ypl - (xt[5:6, :] + sy))
        if keep is not None:
            gy = jnp.where(keep, gy, 0.0)
        xrow = jnp.broadcast_to(xt[4:5, :] + sx, (CY, TILE))
        parts = [hi_lo(gy * xt[c : c + 1, :]) for c in range(4)]
        for xx in range(BX):
            m = jnp.where(xrow == (x0 + xx).astype(jnp.float32), 1.0, 0.0).astype(jnp.bfloat16)
            for c in range(4):
                rows = slice((xx * 4 + c) * CY, (xx * 4 + c + 1) * CY)
                amat[rows, 0:TILE] = parts[c][0] * m
                amat[rows, TILE : 2 * TILE] = parts[c][1] * m

    def visit(entries, valid):
        for j, (i, n, x0) in enumerate(entries):
            factors(i, n, x0, amats[j], zmats[j], None if j == 0 else j < valid)
        for j, (i, n, x0) in enumerate(entries):
            part = jnp.dot(amats[j][...], zmats[j][...], preferred_element_type=jnp.float32)
            acc[pl.ds(x0, BX)] += part.reshape(BX, 4 * CY, NZ)

    in_groups(list_ref, 0, GROUP_D, BX, visit)


def spread_own_kernel(list_ref, tab_ref, pick_ref, out_ref, acc, sem, *mats):
    def clear(i, _):
        acc[i] = jnp.zeros(acc.shape[1:], jnp.float32)
        return 0

    lax.fori_loop(0, XROWS, clear, 0)
    accumulate(list_ref, tab_ref, pick_ref, acc, mats[:GROUP_D], mats[GROUP_D:])
    copy = pltpu.make_async_copy(acc, out_ref, sem)
    copy.start()
    copy.wait()


def sampled(list_ref, part, tab_ref, pick_ref, fmat, out_ref):
    scale = float(SCALE)
    out_ref[...] = jnp.zeros(out_ref.shape, jnp.float32)

    def contribution(i, n, x0):
        xt, sx, sy = framed(tab_ref, i, n)
        cols = columns(xt, pick_ref[...])
        xrep, yrep, zrep = (cols[:, 128 * k : 128 * (k + 1)] for k in (2, 1, 0))
        lane_i = lax.broadcasted_iota(jnp.int32, (TILE, 128), 1)
        lane = lane_i.astype(jnp.float32)
        xpl = (lane_i // CY).astype(jnp.float32)
        ypl = (lane_i % CY).astype(jnp.float32)
        wy = gauss(ypl - (yrep + sy)) * scale
        xoff = xrep - xpl
        near, far = (
            hi_lo(jnp.where(xoff == (x0 + k * BX).astype(jnp.float32) - sx, wy, 0.0)) for k in range(2)
        )
        f = fmat[pl.ds(x0, 2 * BX)].reshape(2 * BP, 3 * NZ)
        coarse, fine = (jnp.concatenate([near[k], far[k]], axis=1) for k in range(2))
        g = jnp.dot(jnp.concatenate([coarse, fine], axis=0), f, preferred_element_type=jnp.float32)
        g = g[:TILE] + g[TILE:]
        sums = [None] * 3
        for q in range(NZ // 128):
            wz = gauss(lane + (128.0 * q) - zrep) * scale
            for c in range(3):
                t = g[:, c * NZ + 128 * q : c * NZ + 128 * (q + 1)] * wz
                sums[c] = t if sums[c] is None else sums[c] + t
        return [jnp.sum(v.T, axis=0, keepdims=True) for v in sums]

    def visit(entries, valid):
        got = [contribution(*e) for e in entries]
        for (i, n, x0), rows in zip(entries, got):
            for c in range(3):
                if valid is None:
                    out_ref[i, c : c + 1, :] += rows[c]
                else:
                    out_ref[i, c : c + 1, :] = rows[c]

    in_groups(list_ref, part, GROUP_V, 2 * BX, visit)


def main_kernel(
    units_ref,
    list_ref,
    tab_ref,
    pick_ref,
    field_ref,
    ground_ref,
    old_ref,
    dens_ref,
    out_ref,
    fmat,
    acc,
    sem,
    wide_a,
    wide_b,
    band_ref,
    flow,
    *mats,
):
    step = pl.program_id(0)
    steps = CX // XO

    def filtered(b, wide, chans=(0, 1, 2, 3)):
        base = b * XO
        for q in range(NZ // 128):
            cols = slice(q * 128, (q + 1) * 128)
            for c in chans:
                outs = x_filtered(lambda i: acc[base + i, c * CY : (c + 1) * CY, cols], RAW, XO)
                for o in range(XO):
                    hi, lo = hi_lo(outs[o])
                    rows = slice((c * XO + o) * CY, (c * XO + o + 1) * CY)
                    wide[0, rows, cols] = hi
                    wide[1, rows, cols] = lo

    def finish(b, wide, h):
        cols = slice(h * 256, (h + 1) * 256)
        zs = slice(h * 128, h * 128 + ZW)
        full = jnp.concatenate([wide[0, :, zs], wide[0, :, zs], wide[1, :, zs]], axis=1)
        dens = jnp.dot(full, band_ref[h], preferred_element_type=jnp.float32)
        dens = dens.reshape(4, XO, CY, 256)
        dens_ref[3, :, :, cols] = dens[3]
        for c in range(3):
            d = dens[c] + dens[3] * field_ref[c : c + 1, cols][None]
            dens_ref[c, :, :, cols] = d
            flow[c, pl.ds(12 + b * XO, XO), :, cols] = d + ground_ref[c : c + 1, cols][None]

    @pl.when(step == 0)
    def _():
        copy = pltpu.make_async_copy(old_ref, acc, sem)
        copy.start()

        def clear(i, _):
            flow[:, i] = jnp.zeros((3, CY, NZ), jnp.float32)
            flow[:, 12 + CX + i] = jnp.zeros((3, CY, NZ), jnp.float32)
            return 0

        lax.fori_loop(0, 16, clear, 0)
        for i in range(BUCKETS * BX, FROWS):
            fmat[i] = jnp.zeros(fmat.shape[1:], jnp.bfloat16)
        for h in range(2):
            for q in range(3):
                row = lax.broadcasted_iota(jnp.int32, (128, 256), 0) + 128 * (q + h)
                col = lax.broadcasted_iota(jnp.int32, (128, 256), 1) + 256 * h
                hi, lo = hi_lo(gauss((row - col).astype(jnp.float32)))
                band_ref[h, q * 128 : (q + 1) * 128, :] = hi
                band_ref[h, ZW + q * 128 : ZW + (q + 1) * 128, :] = lo
                band_ref[h, 2 * ZW + q * 128 : 2 * ZW + (q + 1) * 128, :] = hi
        copy.wait()
        accumulate(units_ref, tab_ref, pick_ref, acc, mats[:GROUP_D], mats[GROUP_D:])
        filtered(0, wide_a)

    for parity, now, later in ((1, wide_a, wide_b), (0, wide_b, wide_a)):

        @pl.when((step > 0) & (step <= steps) & (step % 2 == parity))
        def _(now=now, later=later):
            ahead = jnp.minimum(step, steps - 1)
            finish(step - 1, now, 0)
            filtered(ahead, later, (0, 1))
            finish(step - 1, now, 1)
            filtered(ahead, later, (2, 3))

    @pl.when(step > steps)
    def _():
        def block(b, _):
            for c in range(3):
                for j in range(NZ // 128):
                    cols = slice(j * 128, (j + 1) * 128)
                    outs = x_filtered(lambda i: flow[c, b * BX + i, :, cols], UNIT, BX)
                    for o in range(BX):
                        fmat[b * BX + o, :, c * NZ + j * 128 : c * NZ + (j + 1) * 128] = outs[o].astype(jnp.bfloat16)
            return 0

        lax.fori_loop(0, BUCKETS, block, 0)
        sampled(list_ref, 0, tab_ref, pick_ref, fmat, out_ref)


def sample_own_kernel(part, list_ref, tab_ref, pick_ref, fmat, out_ref):
    sampled(list_ref, part, tab_ref, pick_ref, fmat, out_ref)


def smem():
    return pl.BlockSpec(memory_space=pltpu.SMEM)


def whole(shape):
    return pl.BlockSpec(shape, lambda i: (0,) * len(shape))


PARAMS = pltpu.CompilerParams(vmem_limit_bytes=24 << 20)
MAIN_PARAMS = pltpu.CompilerParams(vmem_limit_bytes=40 << 20)


def factor_scratch():
    return [pltpu.VMEM((4 * BP, 2 * TILE), jnp.bfloat16)] * GROUP_D + [
        pltpu.VMEM((2 * TILE, NZ), jnp.bfloat16)
    ] * GROUP_D


def spread_own_call(listing, table, pick):
    return pl.pallas_call(
        spread_own_kernel,
        grid=(1,),
        in_specs=[smem(), whole(table.shape), whole(pick.shape)],
        out_specs=pl.BlockSpec(memory_space=pltpu.HBM),
        out_shape=pltpu.HBM((XROWS, 4 * CY, NZ), jnp.float32),
        scratch_shapes=[pltpu.VMEM((XROWS, 4 * CY, NZ), jnp.float32), pltpu.SemaphoreType.DMA] + factor_scratch(),
        compiler_params=PARAMS,
        cost_estimate=pl.CostEstimate(flops=10**10, transcendentals=0, bytes_accessed=3 * 10**7),
        name="spread_own",
    )(listing, table, pick)


def main_call(units, listing, table, pick, field, ground, old):
    steps = CX // XO
    n = table.shape[0]
    fshape = (FROWS, CY, 3 * NZ)
    return pl.pallas_call(
        main_kernel,
        grid=(steps + 2,),
        in_specs=[smem()] * 2
        + [whole(v.shape) for v in (table, pick, field, ground)]
        + [pl.BlockSpec(memory_space=pltpu.HBM)],
        out_specs=[
            pl.BlockSpec((4, XO, CY, NZ), lambda i: (0, jnp.clip(i - 1, 0, steps - 1), 0, 0)),
            whole((n, 8, TILE)),
            whole(fshape),
        ],
        out_shape=[
            jax.ShapeDtypeStruct((4, CX, CY, NZ), jnp.float32),
            jax.ShapeDtypeStruct((n, 8, TILE), jnp.float32),
            jax.ShapeDtypeStruct(fshape, jnp.bfloat16),
        ],
        scratch_shapes=[
            pltpu.VMEM(old.shape, jnp.float32),
            pltpu.SemaphoreType.DMA,
            pltpu.VMEM((2, 4 * XO * CY, NZ), jnp.bfloat16),
            pltpu.VMEM((2, 4 * XO * CY, NZ), jnp.bfloat16),
            pltpu.VMEM((2, 3 * ZW, 256), jnp.bfloat16),
            pltpu.VMEM((3, BUCKETS * BX + 12, CY, NZ), jnp.float32),
        ]
        + factor_scratch(),
        compiler_params=MAIN_PARAMS,
        cost_estimate=pl.CostEstimate(flops=4 * 10**10, transcendentals=0, bytes_accessed=6 * 10**7),
        name="main",
    )(units, listing, table, pick, field, ground, old)


def sample_own_call(part, listing, table, pick, fmat):
    n = table.shape[0]

    def kernel(*refs):
        sample_own_kernel(part, *refs)

    return pl.pallas_call(
        kernel,
        grid=(1,),
        in_specs=[smem(), whole(table.shape), whole(pick.shape), whole(fmat.shape)],
        out_specs=whole((n, 8, TILE)),
        out_shape=jax.ShapeDtypeStruct((n, 8, TILE), jnp.float32),
        compiler_params=PARAMS,
        cost_estimate=pl.CostEstimate(flops=10**10, transcendentals=0, bytes_accessed=3 * 10**7),
        name="sample_own",
    )(listing, table, pick, fmat)


def reached(x, y, exists, sx, sy):
    ax, ay = x + sx, y + sy
    near = (ax >= 0) & (ax < CX + 2 * REACH) & (ay >= -REACH) & (ay < CY + REACH) & exists
    lo = jnp.min(jnp.where(near, ax, 127), axis=-1).reshape(-1)
    hi = jnp.max(jnp.where(near, ax, -1), axis=-1).reshape(-1)
    return lo, hi


def listed(at, lo, hi, per):
    active = lo <= hi
    k = jnp.arange(lo.shape[0] + 2, dtype=jnp.int32)
    i = k[:-2]
    pos = jnp.sum((i[None, :] < i[:, None]) & active[None, :], axis=1, dtype=jnp.int32)
    code = jnp.where(active, (at * 128 + lo) * 128 + hi, 0)
    spot = jnp.where(active, pos + 2, -1)
    grid = jnp.where(spot[None, :] == k[:, None], code[None, :], 0)
    grid = jnp.where(k[:, None] == 1, active[None, :].astype(jnp.int32), grid)
    return jnp.sum(grid, axis=1) + jnp.where(k == 0, per, 0)


def both_lists(lo, hi, per):
    at = jnp.arange(lo.shape[0], dtype=jnp.int32)
    split = listed(
        jnp.concatenate([at, at]),
        jnp.concatenate([lo, lo + BX]),
        jnp.concatenate([jnp.minimum(hi, lo + BX - 1), hi]),
        per,
    )
    return split, listed(at, lo, hi, per)


def ring(value, steps):
    count = lax.axis_size("stream")
    return lax.ppermute(value, "stream", [(i, (i + steps) % count) for i in range(count)])


def line(value, steps):
    count = lax.axis_size("span")
    first, last = max(0, -steps), min(count, count - steps)
    return lax.ppermute(value, "span", [(i, i + steps) for i in range(first, last)])


def on_device(records, cells, counts, background, field):
    cap = records.shape[3]
    total = 9 * cap
    tiles = total // TILE
    bf16, f32 = jnp.bfloat16, jnp.float32
    slots = jnp.arange(cap, dtype=jnp.int32)
    live = slots[None, :] < counts[0][:, None]
    cell = cells[0]
    z = cell % NZ
    x = jnp.where(live, cell // (CY * NZ), 255)
    y = (cell // NZ) % CY
    row = jnp.arange(8)[None, :, None]
    places = jnp.where(row == 4, x[:, None], jnp.where(row == 5, y[:, None], jnp.where(row == 6, z[:, None] // 16, z[:, None] % 16)))
    outgoing = jnp.where(row < 4, jnp.pad(records[0], ((0, 0), (0, 4), (0, 0))), places.astype(bf16))
    outgoing = outgoing.reshape(3, 3, 8, cap)
    dead = jnp.zeros((8,), bf16).at[4].set(255)[:, None]
    outgoing = jnp.stack([ring(outgoing[0], -1), outgoing[1], ring(outgoing[2], 1)])
    me = lax.axis_index("span")
    spans = lax.axis_size("span")
    has_low, has_high = me > 0, me < spans - 1
    from_high = jnp.where(has_high, line(outgoing[:, 0], -1), dead)
    from_low = jnp.where(has_low, line(outgoing[:, 2], 1), dead)
    inbound = jnp.stack([from_high, outgoing[:, 1], from_low], axis=1)
    inbound = inbound.transpose(2, 0, 1, 3).reshape(8, total)

    gi = inbound[4:].astype(jnp.int32)
    gx, gy, gz = gi[0], gi[1], gi[2] * 16 + gi[3]
    klass = (gy >= REACH).astype(jnp.int32) + (gy >= CY - REACH)
    klass = jnp.where(gx > 200, 3, klass)
    kx = jnp.where(klass == 1, CX - 1 - gx, gx)
    key = ((klass * 256 + kx) * CY + gy) * NZ + gz
    order = jnp.arange(total, dtype=jnp.int32)
    key, order, *vals = lax.sort((key, order) + tuple(inbound[c].astype(f32) for c in range(4)), num_keys=1)
    sz = key % NZ
    sy = key // NZ % CY
    sx = key // (CY * NZ) % 256
    sx = jnp.where(key // (CY * NZ * 256) == 1, CX - 1 - sx, sx)
    packed = jnp.stack(vals + [v.astype(f32) for v in (sx, sy, sz // 16, sz % 16)]).astype(bf16)
    packed = packed.reshape(8, tiles, TILE).transpose(1, 0, 2)

    low = line(packed, 1)
    high = line(packed, -1)
    tx, ty = sx.reshape(tiles, TILE), sy.reshape(tiles, TILE)
    own_units, own_list = both_lists(*reached(tx, ty, tx < 200, REACH, 0), 0)
    three, own_units = lax.optimization_barrier((jnp.stack([low, packed, high]), own_units))
    arrays = jnp.stack([ring(three, 1), three, ring(three, -1)])
    places = arrays[:, :, :, 4:6].astype(jnp.int32)
    shift = jnp.arange(-1, 2, dtype=jnp.int32)
    exists = jnp.stack([has_low, jnp.array(True), has_high])
    exists = exists[None, :] & ~((shift[:, None] == 0) & (shift[None, :] == 0))
    lo, hi = reached(
        places[:, :, :, 0],
        places[:, :, :, 1],
        exists[:, :, None, None],
        CX * shift[:, None, None, None] + REACH,
        CY * shift[None, :, None, None],
    )
    rest_units, rest_list = both_lists(lo, hi, tiles)
    table = arrays.reshape(9 * tiles, 8, TILE)

    pick = jnp.asarray(PICK, bf16)
    half = spread_own_call(own_units, packed, pick)
    density, partial, fmat = main_call(rest_units, rest_list, table, pick, field, background, half)
    early = sample_own_call(1, own_list, packed, pick, fmat)
    partial = partial[:, :3].reshape(3, 3, tiles, 3, TILE)
    mixed = partial[1] + ring(partial[2], 1) + ring(partial[0], -1)
    mixed, own_list = lax.optimization_barrier((mixed, own_list))
    late = sample_own_call(2, own_list, packed, pick, fmat)
    mine = (early + late)[:, :3]
    own = mixed[1] + mine + line(mixed[2], 1) + line(mixed[0], -1)
    own = own.transpose(1, 0, 2).reshape(3, total)
    _, *vel = lax.sort((order, own[0], own[1], own[2]), num_keys=1)
    velocity = jnp.stack([v.reshape(9, cap) for v in vel], axis=1)[None]
    return density, velocity


def solution(mesh):
    return jax.shard_map(
        on_device,
        mesh=mesh,
        in_specs=(
            P(("stream", "span"), None, None, None),
            P(("stream", "span"), None, None),
            P(("stream", "span"), None),
            P(),
            P(),
        ),
        out_specs=(P(None, "stream", "span", None), P(("stream", "span"), None, None, None)),
        check_vma=False,
    )
```

```python
import jax
import jax.numpy as jnp
import numpy as np
from jax import lax
from jax.experimental import pallas as pl
from jax.experimental.pallas import tpu as pltpu
from jax.sharding import PartitionSpec as P

CX = 64
CY = 16
NZ = 512
REACH = 6
TILE = 128
BX = 8
XO = 8
XROWS = 84
BUCKETS = 10
FROWS = 92
ZW = 384
GROUP_D = 5
GROUP_V = 4
BP = BX * CY

spread_width = 12.5


OFFSETS = np.arange(-6, 7).astype(np.float32)
RAW = np.exp(-OFFSETS * OFFSETS / np.float32(spread_width))
SCALE = np.float32(1.0) / np.sum(RAW)
UNIT = RAW * SCALE
PICK = np.zeros((8, 384), np.float32)
PICK[6, :128], PICK[7, :128], PICK[5, 128:256], PICK[4, 256:] = 16.0, 1.0, 1.0, 1.0


def gauss(d):
    return jnp.where(jnp.abs(d) < REACH + 0.5, jnp.exp(d * d * (-1.0 / spread_width)), 0.0)


def hi_lo(v):
    hi = v.astype(jnp.bfloat16)
    lo = (v - hi.astype(jnp.float32)).astype(jnp.bfloat16)
    return hi, lo


def columns(xt, pick):
    return lax.dot_general(
        xt.astype(jnp.bfloat16), pick, (((0,), (0,)), ((), ())), preferred_element_type=jnp.float32
    )


def x_filtered(load, taps, count):
    taps = [float(t) for t in taps]
    outs = []
    ins = [load(i) for i in range(count + 12)]
    for o in range(count):
        total = taps[6] * ins[o + 6]
        for k in range(1, 7):
            total = total + taps[6 + k] * (ins[o + 6 - k] + ins[o + 6 + k])
        outs.append(total)
    return outs


def tile_codes(list_ref, k):
    code = list_ref[k + 2]
    i = code >> 14
    per = list_ref[0]
    n = jnp.where(per == 0, 4, lax.div(i, jnp.maximum(per, 1)))
    return i, n, (code >> 7) & 127, code & 127


def in_groups(list_ref, part, size, width, visit):
    count = list_ref[1]
    middle = (count + 1) // 2
    begin = middle if part == 2 else 0
    end = middle if part == 1 else count

    def group(p, _):
        k = begin + size * p
        visit([tile_codes(list_ref, jnp.minimum(k + j, end - 1))[:3] for j in range(size)], end - k)

        def leftover(t, _):
            i, n, first, last = tile_codes(list_ref, k + t)

            def window(w, _):
                visit([(i, n, first + w * width)], None)
                return 0

            lax.fori_loop(1, (last - first) // width + 1, window, 0)
            return 0

        lax.fori_loop(0, jnp.minimum(end - k, size), leftover, 0)
        return 0

    lax.fori_loop(0, (end - begin + size - 1) // size, group, 0)


def framed(tab_ref, i, n):
    xt = tab_ref[i].astype(jnp.float32)
    row, col = lax.div(n, 3), lax.rem(n, 3)
    sx = ((row - 1) * CX + REACH).astype(jnp.float32)
    sy = ((col - 1) * CY).astype(jnp.float32)
    return xt, sx, sy


def accumulate(list_ref, tab_ref, pick_ref, acc, amats, zmats):
    def factors(i, n, x0, amat, zmat, keep):
        xt, sx, sy = framed(tab_ref, i, n)
        zrep = columns(xt, pick_ref[:, 0:128])
        lane = lax.broadcasted_iota(jnp.int32, (TILE, 128), 1).astype(jnp.float32)
        for q in range(NZ // 128):
            hit = jnp.where(lane + (128.0 * q) == zrep, 1.0, 0.0).astype(jnp.bfloat16)
            cols = slice(128 * q, 128 * (q + 1))
            zmat[0:TILE, cols] = hit
            zmat[TILE : 2 * TILE, cols] = hit
        ypl = lax.broadcasted_iota(jnp.int32, (CY, TILE), 0).astype(jnp.float32)
        gy = gauss(ypl - (xt[5:6, :] + sy))
        if keep is not None:
            gy = jnp.where(keep, gy, 0.0)
        xrow = jnp.broadcast_to(xt[4:5, :] + sx, (CY, TILE))
        parts = [hi_lo(gy * xt[c : c + 1, :]) for c in range(4)]
        for xx in range(BX):
            m = jnp.where(xrow == (x0 + xx).astype(jnp.float32), 1.0, 0.0).astype(jnp.bfloat16)
            for c in range(4):
                rows = slice((xx * 4 + c) * CY, (xx * 4 + c + 1) * CY)
                amat[rows, 0:TILE] = parts[c][0] * m
                amat[rows, TILE : 2 * TILE] = parts[c][1] * m

    def visit(entries, valid):
        for j, (i, n, x0) in enumerate(entries):
            factors(i, n, x0, amats[j], zmats[j], None if j == 0 else j < valid)
        for j, (i, n, x0) in enumerate(entries):
            part = jnp.dot(amats[j][...], zmats[j][...], preferred_element_type=jnp.float32)
            acc[pl.ds(x0, BX)] += part.reshape(BX, 4 * CY, NZ)

    in_groups(list_ref, 0, GROUP_D, BX, visit)


def spread_own_kernel(list_ref, tab_ref, pick_ref, out_ref, acc, sem, *mats):
    def clear(i, _):
        acc[i] = jnp.zeros(acc.shape[1:], jnp.float32)
        return 0

    lax.fori_loop(0, XROWS, clear, 0)
    accumulate(list_ref, tab_ref, pick_ref, acc, mats[:GROUP_D], mats[GROUP_D:])
    copy = pltpu.make_async_copy(acc, out_ref, sem)
    copy.start()
    copy.wait()


def sampled(list_ref, part, tab_ref, pick_ref, fmat, out_ref):
    scale = float(SCALE)
    out_ref[...] = jnp.zeros(out_ref.shape, jnp.float32)

    def contribution(i, n, x0):
        xt, sx, sy = framed(tab_ref, i, n)
        cols = columns(xt, pick_ref[...])
        xrep, yrep, zrep = (cols[:, 128 * k : 128 * (k + 1)] for k in (2, 1, 0))
        lane_i = lax.broadcasted_iota(jnp.int32, (TILE, 128), 1)
        lane = lane_i.astype(jnp.float32)
        xpl = (lane_i // CY).astype(jnp.float32)
        ypl = (lane_i % CY).astype(jnp.float32)
        wy = gauss(ypl - (yrep + sy)) * scale
        xoff = xrep - xpl
        near, far = (
            hi_lo(jnp.where(xoff == (x0 + k * BX).astype(jnp.float32) - sx, wy, 0.0)) for k in range(2)
        )
        f = fmat[pl.ds(x0, 2 * BX)].reshape(2 * BP, 3 * NZ)
        coarse, fine = (jnp.concatenate([near[k], far[k]], axis=1) for k in range(2))
        g = jnp.dot(jnp.concatenate([coarse, fine], axis=0), f, preferred_element_type=jnp.float32)
        g = g[:TILE] + g[TILE:]
        sums = [None] * 3
        for q in range(NZ // 128):
            wz = gauss(lane + (128.0 * q) - zrep) * scale
            for c in range(3):
                t = g[:, c * NZ + 128 * q : c * NZ + 128 * (q + 1)] * wz
                sums[c] = t if sums[c] is None else sums[c] + t
        return [jnp.sum(v.T, axis=0, keepdims=True) for v in sums]

    def visit(entries, valid):
        got = [contribution(*e) for e in entries]
        for (i, n, x0), rows in zip(entries, got):
            for c in range(3):
                if valid is None:
                    out_ref[i, c : c + 1, :] += rows[c]
                else:
                    out_ref[i, c : c + 1, :] = rows[c]

    in_groups(list_ref, part, GROUP_V, 2 * BX, visit)


def main_kernel(
    units_ref,
    list_ref,
    tab_ref,
    pick_ref,
    field_ref,
    ground_ref,
    old_ref,
    dens_ref,
    out_ref,
    fmat,
    acc,
    sem,
    wide_a,
    wide_b,
    band_ref,
    flow,
    *mats,
):
    step = pl.program_id(0)
    steps = CX // XO

    def filtered(b, wide, chans=(0, 1, 2, 3)):
        base = b * XO
        for q in range(NZ // 128):
            cols = slice(q * 128, (q + 1) * 128)
            for c in chans:
                outs = x_filtered(lambda i: acc[base + i, c * CY : (c + 1) * CY, cols], RAW, XO)
                for o in range(XO):
                    hi, lo = hi_lo(outs[o])
                    rows = slice((c * XO + o) * CY, (c * XO + o + 1) * CY)
                    wide[0, rows, cols] = hi
                    wide[1, rows, cols] = lo

    def finish(b, wide, h):
        cols = slice(h * 256, (h + 1) * 256)
        zs = slice(h * 128, h * 128 + ZW)
        full = jnp.concatenate([wide[0, :, zs], wide[0, :, zs], wide[1, :, zs]], axis=1)
        dens = jnp.dot(full, band_ref[h], preferred_element_type=jnp.float32)
        dens = dens.reshape(4, XO, CY, 256)
        dens_ref[3, :, :, cols] = dens[3]
        for c in range(3):
            d = dens[c] + dens[3] * field_ref[c : c + 1, cols][None]
            dens_ref[c, :, :, cols] = d
            flow[c, pl.ds(12 + b * XO, XO), :, cols] = d + ground_ref[c : c + 1, cols][None]

    @pl.when(step == 0)
    def _():
        copy = pltpu.make_async_copy(old_ref, acc, sem)
        copy.start()

        def clear(i, _):
            flow[:, i] = jnp.zeros((3, CY, NZ), jnp.float32)
            flow[:, 12 + CX + i] = jnp.zeros((3, CY, NZ), jnp.float32)
            return 0

        lax.fori_loop(0, 16, clear, 0)
        for i in range(BUCKETS * BX, FROWS):
            fmat[i] = jnp.zeros(fmat.shape[1:], jnp.bfloat16)
        for h in range(2):
            for q in range(3):
                row = lax.broadcasted_iota(jnp.int32, (128, 256), 0) + 128 * (q + h)
                col = lax.broadcasted_iota(jnp.int32, (128, 256), 1) + 256 * h
                hi, lo = hi_lo(gauss((row - col).astype(jnp.float32)))
                band_ref[h, q * 128 : (q + 1) * 128, :] = hi
                band_ref[h, ZW + q * 128 : ZW + (q + 1) * 128, :] = lo
                band_ref[h, 2 * ZW + q * 128 : 2 * ZW + (q + 1) * 128, :] = hi
        copy.wait()
        accumulate(units_ref, tab_ref, pick_ref, acc, mats[:GROUP_D], mats[GROUP_D:])
        filtered(0, wide_a)

    for parity, now, later in ((1, wide_a, wide_b), (0, wide_b, wide_a)):

        @pl.when((step > 0) & (step <= steps) & (step % 2 == parity))
        def _(now=now, later=later):
            ahead = jnp.minimum(step, steps - 1)
            finish(step - 1, now, 0)
            filtered(ahead, later, (0, 1))
            finish(step - 1, now, 1)
            filtered(ahead, later, (2, 3))

    @pl.when(step > steps)
    def _():
        def block(b, _):
            for c in range(3):
                for j in range(NZ // 128):
                    cols = slice(j * 128, (j + 1) * 128)
                    outs = x_filtered(lambda i: flow[c, b * BX + i, :, cols], UNIT, BX)
                    for o in range(BX):
                        fmat[b * BX + o, :, c * NZ + j * 128 : c * NZ + (j + 1) * 128] = outs[o].astype(jnp.bfloat16)
            return 0

        lax.fori_loop(0, BUCKETS, block, 0)
        sampled(list_ref, 0, tab_ref, pick_ref, fmat, out_ref)


def sample_own_kernel(part, list_ref, tab_ref, pick_ref, fmat, out_ref):
    sampled(list_ref, part, tab_ref, pick_ref, fmat, out_ref)


def smem():
    return pl.BlockSpec(memory_space=pltpu.SMEM)


def whole(shape):
    return pl.BlockSpec(shape, lambda i: (0,) * len(shape))


PARAMS = pltpu.CompilerParams(vmem_limit_bytes=24 << 20)
MAIN_PARAMS = pltpu.CompilerParams(vmem_limit_bytes=40 << 20)


def factor_scratch():
    return [pltpu.VMEM((4 * BP, 2 * TILE), jnp.bfloat16)] * GROUP_D + [
        pltpu.VMEM((2 * TILE, NZ), jnp.bfloat16)
    ] * GROUP_D


def spread_own_call(listing, table, pick):
    return pl.pallas_call(
        spread_own_kernel,
        grid=(1,),
        in_specs=[smem(), whole(table.shape), whole(pick.shape)],
        out_specs=pl.BlockSpec(memory_space=pltpu.HBM),
        out_shape=pltpu.HBM((XROWS, 4 * CY, NZ), jnp.float32),
        scratch_shapes=[pltpu.VMEM((XROWS, 4 * CY, NZ), jnp.float32), pltpu.SemaphoreType.DMA] + factor_scratch(),
        compiler_params=PARAMS,
        cost_estimate=pl.CostEstimate(flops=10**10, transcendentals=0, bytes_accessed=3 * 10**7),
        name="spread_own",
    )(listing, table, pick)


def main_call(units, listing, table, pick, field, ground, old):
    steps = CX // XO
    n = table.shape[0]
    fshape = (FROWS, CY, 3 * NZ)
    return pl.pallas_call(
        main_kernel,
        grid=(steps + 2,),
        in_specs=[smem()] * 2
        + [whole(v.shape) for v in (table, pick, field, ground)]
        + [pl.BlockSpec(memory_space=pltpu.HBM)],
        out_specs=[
            pl.BlockSpec((4, XO, CY, NZ), lambda i: (0, jnp.clip(i - 1, 0, steps - 1), 0, 0)),
            whole((n, 8, TILE)),
            whole(fshape),
        ],
        out_shape=[
            jax.ShapeDtypeStruct((4, CX, CY, NZ), jnp.float32),
            jax.ShapeDtypeStruct((n, 8, TILE), jnp.float32),
            jax.ShapeDtypeStruct(fshape, jnp.bfloat16),
        ],
        scratch_shapes=[
            pltpu.VMEM(old.shape, jnp.float32),
            pltpu.SemaphoreType.DMA,
            pltpu.VMEM((2, 4 * XO * CY, NZ), jnp.bfloat16),
            pltpu.VMEM((2, 4 * XO * CY, NZ), jnp.bfloat16),
            pltpu.VMEM((2, 3 * ZW, 256), jnp.bfloat16),
            pltpu.VMEM((3, BUCKETS * BX + 12, CY, NZ), jnp.float32),
        ]
        + factor_scratch(),
        compiler_params=MAIN_PARAMS,
        cost_estimate=pl.CostEstimate(flops=4 * 10**10, transcendentals=0, bytes_accessed=6 * 10**7),
        name="main",
    )(units, listing, table, pick, field, ground, old)


def sample_own_call(part, listing, table, pick, fmat):
    n = table.shape[0]

    def kernel(*refs):
        sample_own_kernel(part, *refs)

    return pl.pallas_call(
        kernel,
        grid=(1,),
        in_specs=[smem(), whole(table.shape), whole(pick.shape), whole(fmat.shape)],
        out_specs=whole((n, 8, TILE)),
        out_shape=jax.ShapeDtypeStruct((n, 8, TILE), jnp.float32),
        compiler_params=PARAMS,
        cost_estimate=pl.CostEstimate(flops=10**10, transcendentals=0, bytes_accessed=3 * 10**7),
        name="sample_own",
    )(listing, table, pick, fmat)


def reached(x, y, exists, sx, sy):
    ax, ay = x + sx, y + sy
    near = (ax >= 0) & (ax < CX + 2 * REACH) & (ay >= -REACH) & (ay < CY + REACH) & exists
    lo = jnp.min(jnp.where(near, ax, 127), axis=-1).reshape(-1)
    hi = jnp.max(jnp.where(near, ax, -1), axis=-1).reshape(-1)
    return lo, hi


def listed(at, lo, hi, per):
    active = lo <= hi
    k = jnp.arange(lo.shape[0] + 2, dtype=jnp.int32)
    i = k[:-2]
    pos = jnp.sum((i[None, :] < i[:, None]) & active[None, :], axis=1, dtype=jnp.int32)
    code = jnp.where(active, (at * 128 + lo) * 128 + hi, 0)
    spot = jnp.where(active, pos + 2, -1)
    grid = jnp.where(spot[None, :] == k[:, None], code[None, :], 0)
    grid = jnp.where(k[:, None] == 1, active[None, :].astype(jnp.int32), grid)
    return jnp.sum(grid, axis=1) + jnp.where(k == 0, per, 0)


def both_lists(lo, hi, per):
    at = jnp.arange(lo.shape[0], dtype=jnp.int32)
    split = listed(
        jnp.concatenate([at, at]),
        jnp.concatenate([lo, lo + BX]),
        jnp.concatenate([jnp.minimum(hi, lo + BX - 1), hi]),
        per,
    )
    return split, listed(at, lo, hi, per)


def ring(value, steps):
    count = lax.axis_size("stream")
    return lax.ppermute(value, "stream", [(i, (i + steps) % count) for i in range(count)])


def line(value, steps):
    count = lax.axis_size("span")
    first, last = max(0, -steps), min(count, count - steps)
    return lax.ppermute(value, "span", [(i, i + steps) for i in range(first, last)])


def on_device(records, cells, counts, background, field):
    cap = records.shape[3]
    total = 9 * cap
    tiles = total // TILE
    bf16, f32 = jnp.bfloat16, jnp.float32
    slots = jnp.arange(cap, dtype=jnp.int32)
    live = slots[None, :] < counts[0][:, None]
    cell = cells[0]
    z = cell % NZ
    x = jnp.where(live, cell // (CY * NZ), 255)
    y = (cell // NZ) % CY
    row = jnp.arange(8)[None, :, None]
    places = jnp.where(row == 4, x[:, None], jnp.where(row == 5, y[:, None], jnp.where(row == 6, z[:, None] // 16, z[:, None] % 16)))
    outgoing = jnp.where(row < 4, jnp.pad(records[0], ((0, 0), (0, 4), (0, 0))), places.astype(bf16))
    outgoing = outgoing.reshape(3, 3, 8, cap)
    dead = jnp.zeros((8,), bf16).at[4].set(255)[:, None]
    outgoing = jnp.stack([ring(outgoing[0], -1), outgoing[1], ring(outgoing[2], 1)])
    me = lax.axis_index("span")
    spans = lax.axis_size("span")
    has_low, has_high = me > 0, me < spans - 1
    from_high = jnp.where(has_high, line(outgoing[:, 0], -1), dead)
    from_low = jnp.where(has_low, line(outgoing[:, 2], 1), dead)
    inbound = jnp.stack([from_high, outgoing[:, 1], from_low], axis=1)
    inbound = inbound.transpose(2, 0, 1, 3).reshape(8, total)

    gi = inbound[4:].astype(jnp.int32)
    gx, gy, gz = gi[0], gi[1], gi[2] * 16 + gi[3]
    klass = (gy >= REACH).astype(jnp.int32) + (gy >= CY - REACH)
    klass = jnp.where(gx > 200, 3, klass)
    kx = jnp.where(klass == 1, CX - 1 - gx, gx)
    key = ((klass * 256 + kx) * CY + gy) * NZ + gz
    order = jnp.arange(total, dtype=jnp.int32)
    key, order, *vals = lax.sort((key, order) + tuple(inbound[c].astype(f32) for c in range(4)), num_keys=1)
    sz = key % NZ
    sy = key // NZ % CY
    sx = key // (CY * NZ) % 256
    sx = jnp.where(key // (CY * NZ * 256) == 1, CX - 1 - sx, sx)
    packed = jnp.stack(vals + [v.astype(f32) for v in (sx, sy, sz // 16, sz % 16)]).astype(bf16)
    packed = packed.reshape(8, tiles, TILE).transpose(1, 0, 2)

    low = line(packed, 1)
    high = line(packed, -1)
    tx, ty = sx.reshape(tiles, TILE), sy.reshape(tiles, TILE)
    own_units, own_list = both_lists(*reached(tx, ty, tx < 200, REACH, 0), 0)
    three, own_units = lax.optimization_barrier((jnp.stack([low, packed, high]), own_units))
    arrays = jnp.stack([ring(three, 1), three, ring(three, -1)])
    places = arrays[:, :, :, 4:6].astype(jnp.int32)
    shift = jnp.arange(-1, 2, dtype=jnp.int32)
    exists = jnp.stack([has_low, jnp.array(True), has_high])
    exists = exists[None, :] & ~((shift[:, None] == 0) & (shift[None, :] == 0))
    lo, hi = reached(
        places[:, :, :, 0],
        places[:, :, :, 1],
        exists[:, :, None, None],
        CX * shift[:, None, None, None] + REACH,
        CY * shift[None, :, None, None],
    )
    rest_units, rest_list = both_lists(lo, hi, tiles)
    table = arrays.reshape(9 * tiles, 8, TILE)

    pick = jnp.asarray(PICK, bf16)
    half = spread_own_call(own_units, packed, pick)
    density, partial, fmat = main_call(rest_units, rest_list, table, pick, field, background, half)
    early = sample_own_call(1, own_list, packed, pick, fmat)
    partial = partial[:, :3].reshape(3, 3, tiles, 3, TILE)
    mixed = partial[1] + ring(partial[2], 1) + ring(partial[0], -1)
    mixed, own_list = lax.optimization_barrier((mixed, own_list))
    late = sample_own_call(2, own_list, packed, pick, fmat)
    mine = (early + late)[:, :3]
    own = mixed[1] + mine + line(mixed[2], 1) + line(mixed[0], -1)
    own = own.transpose(1, 0, 2).reshape(3, total)
    _, *vel = lax.sort((order, own[0], own[1], own[2]), num_keys=1)
    velocity = jnp.stack([v.reshape(9, cap) for v in vel], axis=1)[None]
    return density, velocity


def solution(mesh):
    return jax.shard_map(
        on_device,
        mesh=mesh,
        in_specs=(
            P(("stream", "span"), None, None, None),
            P(("stream", "span"), None, None),
            P(("stream", "span"), None),
            P(),
            P(),
        ),
        out_specs=(P(None, "stream", "span", None), P(("stream", "span"), None, None, None)),
        check_vma=False,
    )
```
